1024 devices in a mesh: gx: 16 (over z, x_hi), gy: 8 (over x_lo, core), gz: 8 (over y).
Axes of the slice: x: 8 (x_hi: 2, x_lo: 4; x = x_hi * 4 + x_lo), y: 8, z: 8, core: 2. Of those that a mesh axis runs over, the one named last changes fastest.
Arguments:
- terminal_adjoint: float32 [5, 128, 64, 1024], P(None, 'gx', 'gy', 'gz'), may hold values from -6 to 6
- density: float32 [128, 64, 1024], P('gx', 'gy', 'gz'), may hold values from 0.7 to 1.5
- velocity: float32 [3, 128, 64, 1024], P(None, 'gx', 'gy', 'gz'), may hold values from -0.5 to 0.5
- stiffness: float32 [128, 64, 1024], P('gx', 'gy', 'gz'), may hold values from 0.6 to 1.6
- sponge: float32 [128, 64, 1024], P('gx', 'gy', 'gz'), may hold values from 0.1 to 3
- source_shape: float32 [128, 64, 1024], P('gx', 'gy', 'gz'), may hold values from -0.1875 to 0.1875
- brick_level: int32 [16, 8, 8], replicated, may hold values from 0 to 1
- brick_patch: int32 [16, 8, 8], replicated, may hold values from 0 to 1023, as said below
- patch_owner: int32 [1024], replicated, may hold values from 0 to 1023, as said below
Outputs:
- adjoint: float32 [5, 128, 64, 1024], P(None, 'gx', 'gy', 'gz')
- patch_gradient: float32 [1024, 40], P(('gx', 'gy', 'gz'))
The draws below stay inside these ranges and needn't reach their ends.
Inputs may be any that keep to these rules, and one draw needn't show every extreme that they name: `brick_patch`: each brick names one patch; a patch may be named by several bricks or by none. `patch_owner`: every device owns exactly one patch.
All inputs are finite; a program needn't handle non-finite values.
Results may differ from the reference program's by a relative error of at most 0.00013.
Values sent between devices are 32-bit elements; how exact they have to be, the bound alone decides.
A program may use at most 32 MiB of HBM per device.

```python
import math
import jax
import jax.numpy as jnp

CX = 8
CY = 8
CZ = 128
BX = 8
BY = 8
BZ = 16
STEPS = 1
NX = 128
NY = 64
NZ = 1024
PATCHES = 1024
KBLOCK = 40
N_GX = 16
N_GY = 8
N_GZ = 8


def joint_routing(key):
    owner = jax.random.permutation(jax.random.fold_in(key, 11), PATCHES).astype(jnp.int32)
    device_patch = jnp.zeros((PATCHES,), jnp.int32).at[owner].set(jnp.arange(PATCHES, dtype=jnp.int32))
    bricks = jnp.arange(PATCHES, dtype=jnp.int32)
    kinds = jax.random.randint(jax.random.fold_in(key, 12), (PATCHES,), 0, 4)
    random_target = jax.random.randint(jax.random.fold_in(key, 13), (PATCHES,), 0, PATCHES)
    half_count = PATCHES // 2
    target = jnp.where(kinds == 0, bricks, jnp.where(kinds == 1, (bricks + half_count) % PATCHES, jnp.where(kinds == 2, (bricks + 1) % PATCHES, random_target)))
    target = target.at[half_count].set(0).at[1].set(0).at[2].set(3)
    return (owner, device_patch[target].astype(jnp.int32))


def draw_patch_owner(key, part):
    owner, patches = joint_routing(key)
    return owner


def draw_brick_patch(key, part):
    owner, patches = joint_routing(key)
    return patches.reshape(N_GX, N_GY, N_GZ)


def set_ends(result, key, smallest, high):
    index_at = [jax.random.randint(jax.random.fold_in(key, axis), (), 0, length) for axis, length in enumerate(result.shape)]
    main_axis = result.shape.index(max(result.shape))
    next_to = index_at[:main_axis] + [(index_at[main_axis] + 1) % result.shape[main_axis]] + index_at[main_axis + 1:]
    return result.at[tuple(index_at)].set(smallest).at[tuple(next_to)].set(high)


def levels(key, extent, shards, low, largest):
    gain, own = 1.0, jax.random.fold_in(key, 6)
    for axis_at, parts in shards:
        steps = jnp.exp(jax.random.uniform(jax.random.fold_in(own, axis_at), (parts,), jnp.float32, low / len(shards), largest / len(shards)))
        gain = gain * jnp.repeat(steps, extent[axis_at] // parts).reshape([-1 if axis == axis_at else 1 for axis in range(len(extent))])
    return gain


def gaussian(rng, dims, scale, limit, cuts=(), kind=jnp.bfloat16):
    drawn = jax.random.normal(rng, dims, jnp.float32) * scale
    if len(cuts) > 0:
        drawn = levels(rng, dims, cuts, -0.22, 0.18) * drawn
    return jnp.clip(drawn, min=-limit, max=limit).astype(kind)


def setup_inputs(seed: int = 0) -> dict:
    arg_keys = jax.random.split(jax.random.key(seed), 10)
    terminal_adjoint = gaussian(arg_keys[0], (5, NX, NY, NZ), 1.0, 6.0, ((1, 16), (2, 8), (3, 8)), jnp.float32)
    density = jnp.clip(jnp.exp(math.log(1.5) - 0.7621401 * jax.random.uniform(arg_keys[1], (NX, NY, NZ), jnp.float32) ** levels(arg_keys[1], (NX, NY, NZ), ((0, 16), (1, 8), (2, 8)), -0.2, 0.2)), 0.7, 1.5)
    velocity = jnp.clip(jax.random.uniform(arg_keys[2], (3, NX, NY, NZ), jnp.float32, -0.5, 0.5) * levels(arg_keys[2], (3, NX, NY, NZ), ((1, 16), (2, 8), (3, 8)), -0.4, 0.0), -0.5, 0.5)
    stiffness = jnp.clip(jnp.exp(math.log(1.6) - 0.98082923 * jax.random.uniform(arg_keys[3], (NX, NY, NZ), jnp.float32) ** levels(arg_keys[3], (NX, NY, NZ), ((0, 16), (1, 8), (2, 8)), -0.2, 0.2)), 0.6, 1.6)
    sponge = jnp.clip(jnp.exp(math.log(3.0) - 3.4011974 * jax.random.uniform(arg_keys[4], (NX, NY, NZ), jnp.float32) ** levels(arg_keys[4], (NX, NY, NZ), ((0, 16), (1, 8), (2, 8)), -0.2, 0.2)), 0.1, 3.0)
    source_shape = gaussian(arg_keys[5], (NX, NY, NZ), (BX * BY * BZ) ** -0.5, 0.1875, ((0, 16), (1, 8), (2, 8)), jnp.float32)
    brick_level = set_ends(jax.random.randint(arg_keys[6], (N_GX, N_GY, N_GZ), 0, 2), jax.random.fold_in(arg_keys[6], 1), 0, 1).astype(jnp.int32)
    brick_patch = draw_brick_patch(jax.random.fold_in(arg_keys[9], 71), 0)
    patch_owner = draw_patch_owner(jax.random.fold_in(arg_keys[9], 71), 0)
    return {"terminal_adjoint": terminal_adjoint, "density": density, "velocity": velocity, "stiffness": stiffness, "sponge": sponge, "source_shape": source_shape, "brick_level": brick_level, "brick_patch": brick_patch, "patch_owner": patch_owner}


step_length = 0.14
third = 1.0 / 3.0
two_thirds = 2.0 / 3.0


def transposed_flux(adjoint, density, velocity, stiffness, direction):
    along_speed = velocity[direction]
    components = [along_speed * adjoint[component] for component in range(5)]
    velocity_row = 1 + direction
    components[velocity_row] = components[velocity_row] + density * adjoint[0] + stiffness * adjoint[4]
    components[4] = components[4] + adjoint[velocity_row] / density
    return jnp.stack(components)


def half_inverse_field(brick_level):
    scaled = 0.5 * jnp.exp2(brick_level.astype(jnp.float32))
    spread = jnp.broadcast_to(scaled[:, None, :, None, :, None], (N_GX, CX, N_GY, CY, N_GZ, CZ))
    return spread.reshape(NX, NY, NZ)


def operate(adjoint, density, velocity, stiffness, half_inverse, sponge):
    summed = None
    for direction in range(3):
        partials = half_inverse * transposed_flux(adjoint, density, velocity, stiffness, direction)
        pad_widths = [(0, 0), (0, 0), (0, 0), (0, 0)]
        pad_widths[direction + 1] = (1, 1)
        padded = jnp.pad(partials, pad_widths)
        upper_cut = [slice(None), slice(None), slice(None), slice(None)]
        lower_cut = [slice(None), slice(None), slice(None), slice(None)]
        upper_cut[direction + 1] = slice(2, None)
        lower_cut[direction + 1] = slice(None, -2)
        difference = padded[tuple(upper_cut)] - padded[tuple(lower_cut)]
        summed = difference if summed is None else summed + difference
    return summed - sponge * adjoint


def restrict(adjoint, source_shape):
    weighted = adjoint * source_shape
    boxed = weighted.reshape(5, N_GX, CX // BX, BX, N_GY, CY // BY, BY, N_GZ, CZ // BZ, BZ)
    boxed = jnp.sum(boxed, axis=(3, 6, 9))
    return jnp.transpose(boxed, (1, 3, 5, 0, 2, 4, 6)).reshape(N_GX * N_GY * N_GZ, KBLOCK)


def reference(terminal_adjoint, density, velocity, stiffness, sponge, source_shape, brick_level, brick_patch, patch_owner):
    half_inverse = half_inverse_field(brick_level)
    adjoint = terminal_adjoint

    def apply_op(field_now):
        return operate(field_now, density, velocity, stiffness, half_inverse, sponge)

    blocks = jnp.zeros((PATCHES, KBLOCK), jnp.float32)
    for step_index in range(STEPS):
        section_one = adjoint + step_length * apply_op(adjoint)
        section_two = 0.75 * adjoint + 0.25 * (section_one + step_length * apply_op(section_one))
        adjoint = third * adjoint + two_thirds * (section_two + step_length * apply_op(section_two))
        blocks = blocks + step_length * restrict(adjoint, source_shape)
    patch_sums = jax.ops.segment_sum(blocks, brick_patch.reshape(-1).astype(jnp.int32), num_segments=PATCHES)
    patch_gradient = jnp.zeros_like(patch_sums).at[patch_owner.astype(jnp.int32)].set(patch_sums)
    return adjoint, patch_gradient
```

```python
import functools

import jax
import jax.numpy as jnp
from jax import lax
from jax.experimental import pallas as pl
from jax.experimental.pallas import tpu as pltpu
from jax.sharding import PartitionSpec as P

MESH = pl.DeviceIdType.MESH
F = 5
X = 8
Y = 8
Z = 128
BZ = 16
BOXES = Z // BZ
STAGES = 3
step_length = 0.14
third = 1.0 / 3.0
AXES = ("gx", "gy", "gz")


def kernel(
    sizes,
    level_ref,
    patch_ref,
    owner_ref,
    adjoint_hbm,
    density_hbm,
    velocity_hbm,
    stiffness_hbm,
    sponge_hbm,
    source_hbm,
    out_hbm,
    grad_ref,
    fields,
    density,
    velocity,
    stiffness,
    sponge,
    source,
    speed,
    pull,
    push,
    inverse,
    damp,
    flux_x,
    flux_y,
    send_y,
    send_z,
    halo_x,
    halo_y,
    halo_z,
    result,
    row_send,
    row_recv,
    cell_send,
    cell_recv,
    load_sem,
    store_sem,
    halo_send_sem,
    halo_recv_sem,
    row_send_sem,
    row_recv_sem,
    cell_send_sem,
    cell_recv_sem,
):
    n_gx, n_gy, n_gz = sizes
    gx, gy, gz = (lax.axis_index(axis) for axis in AXES)
    half = lax.rem(gx, 2)
    plane = lax.div(gx, 2)
    n_plane = n_gx // 2
    n_row = 2 * n_gy
    n_cell = n_plane * n_gz
    my_row = half * n_gy + gy
    my_cell = plane * n_gz + gz

    def row_device(t):
        return (plane * 2 + lax.div(t, n_gy), lax.rem(t, n_gy), gz)

    def cell_device(t):
        return (lax.div(t, n_gz) * 2 + half, gy, lax.rem(t, n_gz))

    barrier = pltpu.get_barrier_semaphore()
    me = (gx, gy, gz)
    ups, downs, has_up, has_down = [], [], [], []
    for d in range(3):
        up, down = list(me), list(me)
        up[d] = jnp.minimum(me[d] + 1, sizes[d] - 1)
        down[d] = jnp.maximum(me[d] - 1, 0)
        ups.append(tuple(up))
        downs.append(tuple(down))
        has_up.append(me[d] < sizes[d] - 1)
        has_down.append(me[d] > 0)
    expected = jnp.int32(n_row - 1 + n_cell - 1)
    for d in range(3):
        for has, to in ((has_up[d], ups[d]), (has_down[d], downs[d])):
            expected = expected + jnp.where(has, 1, 0)

            @pl.when(has)
            def _(to=to):
                pl.semaphore_signal(barrier, inc=1, device_id=to, device_id_type=MESH)

    loads = []
    for i, (src, dst) in enumerate(
        (
            (density_hbm, density),
            (velocity_hbm, velocity),
            (stiffness_hbm, stiffness),
            (sponge_hbm, sponge),
            (adjoint_hbm, fields.at[0]),
            (source_hbm, source),
        )
    ):
        copy = pltpu.make_async_copy(src, dst, load_sem.at[i])
        copy.start()
        loads.append(copy)

    def greet_row(r, c):
        pl.semaphore_signal(
            barrier, inc=1, device_id=row_device(lax.rem(my_row + r, n_row)), device_id_type=MESH
        )
        return c

    lax.fori_loop(1, n_row, greet_row, 0)

    def greet_cell(r, c):
        pl.semaphore_signal(
            barrier, inc=1, device_id=cell_device(lax.rem(my_cell + r, n_cell)), device_id_type=MESH
        )
        return c

    lax.fori_loop(1, n_cell, greet_cell, 0)

    for d, halo in enumerate((halo_x, halo_y, halo_z)):
        for side, has in ((0, has_down[d]), (1, has_up[d])):

            @pl.when(jnp.logical_not(has))
            def _(halo=halo, side=side):
                for k in range(STAGES):
                    halo[k, side] = jnp.zeros(halo.shape[2:], jnp.float32)

    level = level_ref[gy, gz, gx]
    scale = 0.5 * step_length * lax.shift_left(jnp.int32(1), level).astype(jnp.float32)
    for copy in loads[:4]:
        copy.wait()
    for x in range(X):
        rho = density[x]
        speed[:, x] = scale * velocity[:, x]
        pull[x] = scale * rho
        push[x] = scale * stiffness[x]
        inverse[x] = scale / rho
        damp[x] = 1.0 - step_length * sponge[x]
    loads[4].wait()

    sub = lax.broadcasted_iota(jnp.int32, (Y, Z), 0)
    lane = lax.broadcasted_iota(jnp.int32, (Y, Z), 1)
    first_y, last_y = sub == 0, sub == Y - 1
    first_z, last_z = lane == 0, lane == Z - 1

    def flux(v, joint, x, d):
        c = speed[d, x]
        q = [c * v[f] for f in range(F)]
        q[1 + d] = q[1 + d] + joint
        q[4] = q[4] + inverse[x] * v[1 + d]
        return q

    def joint_term(v, x):
        return pull[x] * v[0] + push[x] * v[4]

    def halo_copy(k, d, side):
        src = (
            flux_x.at[k, (X - 1) * side],
            send_y.at[k, side],
            send_z.at[k, side],
        )[d]
        dst = (halo_x, halo_y, halo_z)[d].at[k, 1 - side]
        return pltpu.make_async_remote_copy(
            src_ref=src,
            dst_ref=dst,
            send_sem=halo_send_sem.at[k, d, side],
            recv_sem=halo_recv_sem.at[k, d, 1 - side],
            device_id=ups[d] if side else downs[d],
            device_id_type=MESH,
        )

    def send_halo(k, d):
        for side, has in ((1, has_up[d]), (0, has_down[d])):

            @pl.when(has)
            def _(side=side):
                halo_copy(k, d, side).start()

    def wait_halo(k, d):
        for side, has in ((1, has_down[d]), (0, has_up[d])):

            @pl.when(has)
            def _(side=side):
                halo_copy(k, d, side).wait_recv()

    for k in range(STAGES):
        for x in (0, X - 1):
            v = [fields[k, f, x] for f in range(F)]
            q = flux(v, joint_term(v, x), x, 0)
            for f in range(F):
                flux_x[k, x, f] = q[f]
        if k == 0:
            pl.semaphore_wait(barrier, expected)
        send_halo(k, 0)
        packs = [jnp.zeros((Y, Z), jnp.float32), jnp.zeros((Y, Z), jnp.float32)]
        for x in range(X):
            v = [fields[k, f, x] for f in range(F)]
            joint = joint_term(v, x)
            if 0 < x < X - 1:
                q = flux(v, joint, x, 0)
                for f in range(F):
                    flux_x[k, x, f] = q[f]
            q = flux(v, joint, x, 2)
            for f in range(F):
                here = lane == f * X + x
                packs[0] = jnp.where(here, jnp.broadcast_to(q[f][:, 0:1], (Y, Z)), packs[0])
                packs[1] = jnp.where(here, jnp.broadcast_to(q[f][:, Z - 1 : Z], (Y, Z)), packs[1])
                fields[k + 1, f, x] = (
                    damp[x] * v[f]
                    + jnp.where(last_z, 0.0, pltpu.roll(q[f], Z - 1, 1))
                    - jnp.where(first_z, 0.0, pltpu.roll(q[f], 1, 1))
                )
            q = flux(v, joint, x, 1)
            for f in range(F):
                flux_y[k, f, pl.ds(x * Y, Y), :] = q[f]
                fields[k + 1, f, x] += jnp.where(last_y, 0.0, pltpu.roll(q[f], Y - 1, 0)) - jnp.where(
                    first_y, 0.0, pltpu.roll(q[f], 1, 0)
                )
        for side in range(2):
            send_z[k, side] = packs[side]
        send_halo(k, 2)
        for f in range(F):
            for side in range(2):
                send_y[k, side, f] = flux_y[k, f, pl.ds((Y - 1) * side, X, stride=Y), :]
        send_halo(k, 1)
        for x in range(X):
            for f in range(F):
                if x == 0:
                    fields[k + 1, f, x] += flux_x[k, x + 1, f]
                elif x == X - 1:
                    fields[k + 1, f, x] -= flux_x[k, x - 1, f]
                else:
                    fields[k + 1, f, x] += flux_x[k, x + 1, f] - flux_x[k, x - 1, f]
        wait_halo(k, 1)
        wait_halo(k, 2)
        low_z, high_z = halo_z[k, 0], halo_z[k, 1]
        for f in range(F):
            low_y, high_y = halo_y[k, 0, f], halo_y[k, 1, f]
            for x in range(X):
                at = f * X + x
                delta = jnp.where(
                    last_y,
                    jnp.broadcast_to(high_y[x : x + 1], (Y, Z)),
                    jnp.where(first_y, -jnp.broadcast_to(low_y[x : x + 1], (Y, Z)), 0.0),
                )
                delta += jnp.where(
                    last_z,
                    jnp.broadcast_to(high_z[:, at : at + 1], (Y, Z)),
                    jnp.where(first_z, -jnp.broadcast_to(low_z[:, at : at + 1], (Y, Z)), 0.0),
                )
                fields[k + 1, f, x] += delta
        wait_halo(k, 0)
        for f in range(F):
            fields[k + 1, f, 0] -= halo_x[k, 0, f]
            fields[k + 1, f, X - 1] += halo_x[k, 1, f]

    loads[5].wait()
    lines = []
    for f in range(F):
        total = jnp.zeros((Y, Z), jnp.float32)
        for x in range(X):
            value = third * fields[0, f, x] + 0.5 * fields[1, f, x] + (0.5 * third) * fields[3, f, x]
            result[f, x] = value
            total += value * source[x]
        lines.append(jnp.sum(total, axis=0, keepdims=True))
    store = pltpu.make_async_copy(result, out_hbm, store_sem)
    store.start()

    row_lane = lax.broadcasted_iota(jnp.int32, (1, Z), 1)
    block = jnp.zeros((1, Z), jnp.float32)
    for f in range(F):
        line = lines[f]
        for shift in (1, 2, 4, 8):
            line = line + pltpu.roll(line, Z - shift, 1)
        if f:
            line = pltpu.roll(line, f, 1)
        block = jnp.where(lax.rem(row_lane, BZ) == f, line, block)
    block = step_length * block

    def owner_of(i, j, k):
        return owner_ref[patch_ref[j, k, i]]

    def split_owner(o):
        ox = lax.div(o, n_gy * n_gz)
        oy = lax.rem(lax.div(o, n_gz), n_gy)
        oz = lax.rem(o, n_gz)
        return lax.rem(ox, 2) * n_gy + oy, lax.div(ox, 2) * n_gz + oz

    to_row, _ = split_owner(owner_of(gx, gy, gz))
    for t in range(n_row):
        row_send[t] = jnp.where(to_row == t, block, 0.0)

    def row_copy(r):
        t = lax.rem(my_row + r, n_row)
        return pltpu.make_async_remote_copy(
            src_ref=row_send.at[t],
            dst_ref=row_recv.at[my_row],
            send_sem=row_send_sem.at[r],
            recv_sem=row_recv_sem.at[r],
            device_id=row_device(t),
            device_id_type=MESH,
        )

    def loop(n, body):
        def step(r, c):
            body(r)
            return c

        lax.fori_loop(1, n, step, 0)

    loop(n_row, lambda r: row_copy(r).start())
    row_recv[my_row] = row_send[my_row]

    target = jnp.full((1, n_row), -1, jnp.int32)
    at = lax.broadcasted_iota(jnp.int32, (1, n_row), 1)
    for t in range(n_row):
        _, cell = split_owner(owner_of(plane * 2 + t // n_gy, t % n_gy, gz))
        target = jnp.where(at == t, cell, target)
    choose = (lax.broadcasted_iota(jnp.int32, (n_cell, n_row), 0) == target).astype(jnp.float32)
    spread_to = lax.broadcasted_iota(jnp.int32, (Z, Z), 1)
    spread = (
        lax.broadcasted_iota(jnp.int32, (Z, Z), 0)
        == BZ * lax.rem(spread_to, BOXES) + lax.div(spread_to, BOXES)
    ).astype(jnp.float32)

    loop(n_row, lambda r: row_copy(r).wait_recv())
    rows = row_recv[...].reshape(n_row, Z)
    cells = jnp.dot(
        choose, rows, preferred_element_type=jnp.float32, precision=lax.Precision.HIGHEST
    )
    for t in range(n_cell):
        cell_send[t] = cells[t : t + 1]

    def cell_copy(r):
        t = lax.rem(my_cell + r, n_cell)
        return pltpu.make_async_remote_copy(
            src_ref=cell_send.at[t],
            dst_ref=cell_recv.at[my_cell],
            send_sem=cell_send_sem.at[r],
            recv_sem=cell_recv_sem.at[r],
            device_id=cell_device(t),
            device_id_type=MESH,
        )

    loop(n_cell, lambda r: cell_copy(r).start())
    cell_recv[my_cell] = cell_send[my_cell]
    loop(n_cell, lambda r: cell_copy(r).wait_recv())
    own = jnp.sum(cell_recv[...].reshape(n_cell, Z), axis=0, keepdims=True)
    ordered = jnp.dot(
        own, spread, preferred_element_type=jnp.float32, precision=lax.Precision.HIGHEST
    )
    grad_ref[...] = ordered[:, : F * BOXES]

    for k in range(STAGES):
        for d in range(3):
            for side, has in ((1, has_up[d]), (0, has_down[d])):

                @pl.when(has)
                def _(side=side, k=k, d=d):
                    halo_copy(k, d, side).wait_send()

    loop(n_row, lambda r: row_copy(r).wait_send())
    loop(n_cell, lambda r: cell_copy(r).wait_send())
    store.wait()


def solution(mesh):
    sizes = tuple(mesh.shape[axis] for axis in AXES)
    n_row = 2 * sizes[1]
    n_cell = sizes[0] // 2 * sizes[2]

    def body(
        terminal_adjoint,
        density,
        velocity,
        stiffness,
        sponge,
        source_shape,
        brick_level,
        brick_patch,
        patch_owner,
    ):
        f32 = jnp.float32
        smem = pl.BlockSpec(memory_space=pltpu.SMEM)
        hbm = pl.BlockSpec(memory_space=pl.ANY)
        return pl.pallas_call(
            functools.partial(kernel, sizes),
            out_shape=(
                jax.ShapeDtypeStruct((F, X, Y, Z), f32),
                jax.ShapeDtypeStruct((1, F * BOXES), f32),
            ),
            in_specs=[smem] * 3 + [hbm] * 6,
            out_specs=(hbm, pl.BlockSpec(memory_space=pltpu.VMEM)),
            scratch_shapes=[
                pltpu.VMEM((STAGES + 1, F, X, Y, Z), f32),
                pltpu.VMEM((X, Y, Z), f32),
                pltpu.VMEM((3, X, Y, Z), f32),
                pltpu.VMEM((X, Y, Z), f32),
                pltpu.VMEM((X, Y, Z), f32),
                pltpu.VMEM((X, Y, Z), f32),
                pltpu.VMEM((3, X, Y, Z), f32),
                pltpu.VMEM((X, Y, Z), f32),
                pltpu.VMEM((X, Y, Z), f32),
                pltpu.VMEM((X, Y, Z), f32),
                pltpu.VMEM((X, Y, Z), f32),
                pltpu.VMEM((STAGES, X, F, Y, Z), f32),
                pltpu.VMEM((STAGES, F, X * Y, Z), f32),
                pltpu.VMEM((STAGES, 2, F, X, Z), f32),
                pltpu.VMEM((STAGES, 2, Y, Z), f32),
                pltpu.VMEM((STAGES, 2, F, Y, Z), f32),
                pltpu.VMEM((STAGES, 2, F, X, Z), f32),
                pltpu.VMEM((STAGES, 2, Y, Z), f32),
                pltpu.VMEM((F, X, Y, Z), f32),
                pltpu.VMEM((n_row, 1, Z), f32),
                pltpu.VMEM((n_row, 1, Z), f32),
                pltpu.VMEM((n_cell, 1, Z), f32),
                pltpu.VMEM((n_cell, 1, Z), f32),
                pltpu.SemaphoreType.DMA((6,)),
                pltpu.SemaphoreType.DMA,
                pltpu.SemaphoreType.DMA((STAGES, 3, 2)),
                pltpu.SemaphoreType.DMA((STAGES, 3, 2)),
                pltpu.SemaphoreType.DMA((n_row,)),
                pltpu.SemaphoreType.DMA((n_row,)),
                pltpu.SemaphoreType.DMA((n_cell,)),
                pltpu.SemaphoreType.DMA((n_cell,)),
            ],
            compiler_params=pltpu.CompilerParams(collective_id=0, has_side_effects=True),
        )(
            jnp.transpose(brick_level, (1, 2, 0)),
            jnp.transpose(brick_patch, (1, 2, 0)),
            patch_owner,
            terminal_adjoint,
            density,
            velocity,
            stiffness,
            sponge,
            source_shape,
        )

    in_specs = (
        P(None, "gx", "gy", "gz"),
        P("gx", "gy", "gz"),
        P(None, "gx", "gy", "gz"),
        P("gx", "gy", "gz"),
        P("gx", "gy", "gz"),
        P("gx", "gy", "gz"),
        P(),
        P(),
        P(),
    )
    out_specs = (P(None, "gx", "gy", "gz"), P(AXES, None))
    return jax.shard_map(body, mesh=mesh, in_specs=in_specs, out_specs=out_specs, check_vma=False)
```

```python
import functools

import jax
import jax.numpy as jnp
from jax import lax
from jax.experimental import pallas as pl
from jax.experimental.pallas import tpu as pltpu
from jax.sharding import PartitionSpec as P

MESH = pl.DeviceIdType.MESH
F = 5
X = 8
Y = 8
Z = 128
BZ = 16
BOXES = Z // BZ
TILE = 8
STAGES = 3
step_length = 0.14
third = 1.0 / 3.0
AXES = ("gx", "gy", "gz")


def kernel(
    sizes,
    level_ref,
    patch_ref,
    owner_ref,
    adjoint_hbm,
    density_hbm,
    velocity_hbm,
    stiffness_hbm,
    sponge_hbm,
    source_hbm,
    out_hbm,
    grad_ref,
    fields,
    density,
    velocity,
    stiffness,
    sponge,
    source,
    speed,
    pull,
    push,
    inverse,
    damp,
    flux_x,
    flux_y,
    send_y,
    send_z,
    halo_x,
    halo_y,
    halo_z,
    result,
    choose,
    row_choice,
    spread,
    row_send,
    row_recv,
    column_send,
    column_recv,
    plane_send,
    plane_recv,
    load_sem,
    store_sem,
    halo_send_sem,
    halo_recv_sem,
    row_send_sem,
    row_recv_sem,
    column_send_sem,
    column_recv_sem,
    plane_send_sem,
    plane_recv_sem,
):
    n_gx, n_gy, n_gz = sizes
    gx, gy, gz = (lax.axis_index(axis) for axis in AXES)
    half = lax.rem(gx, 2)
    plane = lax.div(gx, 2)
    n_plane = n_gx // 2
    n_row = 2 * n_gy
    my_row = half * n_gy + gy

    def row_device(t):
        return (plane * 2 + lax.div(t, n_gy), lax.rem(t, n_gy), gz)

    def column_device(t):
        return (gx, gy, t)

    def plane_device(t):
        return (t * 2 + half, gy, gz)

    barrier = pltpu.get_barrier_semaphore()
    me = (gx, gy, gz)
    ups, downs, has_up, has_down = [], [], [], []
    for d in range(3):
        up, down = list(me), list(me)
        up[d] = jnp.minimum(me[d] + 1, sizes[d] - 1)
        down[d] = jnp.maximum(me[d] - 1, 0)
        ups.append(tuple(up))
        downs.append(tuple(down))
        has_up.append(me[d] < sizes[d] - 1)
        has_down.append(me[d] > 0)

    def greet(to):
        pl.semaphore_signal(barrier, inc=1, device_id=to, device_id_type=MESH)

    cross_up = jnp.logical_and(half == 1, has_up[0])
    cross_down = jnp.logical_and(half == 0, has_down[0])
    for has, to in ((cross_up, ups[0]), (cross_down, downs[0])):

        @pl.when(has)
        def _(to=to):
            greet(to)

    greeted = []
    for n, mine, device, near in (
        (n_row, my_row, row_device, (1, n_row - 1, n_row // 2)),
        (n_gz, gz, column_device, (1, n_gz - 1)),
    ):
        for r in near:
            greet(device(lax.rem(mine + r, n)))
        greeted.append(near)

    loads = []
    for i, (src, dst) in enumerate(
        (
            (density_hbm, density),
            (velocity_hbm, velocity),
            (stiffness_hbm, stiffness),
            (sponge_hbm, sponge),
            (adjoint_hbm, fields.at[0]),
            (source_hbm, source),
        )
    ):
        copy = pltpu.make_async_copy(src, dst, load_sem.at[i])
        copy.start()
        loads.append(copy)

    for n, mine, device, near in (
        (n_row, my_row, row_device, greeted[0]),
        (n_gz, gz, column_device, greeted[1]),
        (n_plane, plane, plane_device, ()),
    ):
        for r in range(1, n):
            if r not in near:
                greet(device(lax.rem(mine + r, n)))
    expected = (
        jnp.int32(n_row - 1 + n_gz - 1 + n_plane - 1)
        + jnp.where(cross_up, 1, 0)
        + jnp.where(cross_down, 1, 0)
    )

    for d, halo in enumerate((halo_x, halo_y, halo_z)):
        for side, has in ((0, has_down[d]), (1, has_up[d])):

            @pl.when(jnp.logical_not(has))
            def _(halo=halo, side=side):
                for k in range(STAGES):
                    halo[k, side] = jnp.zeros(halo.shape[2:], jnp.float32)

    level = level_ref[gy, gz, gx]
    scale = 0.5 * step_length * lax.shift_left(jnp.int32(1), level).astype(jnp.float32)
    for copy in loads[:4]:
        copy.wait()
    for x in range(X):
        rho = density[x]
        speed[:, x] = scale * velocity[:, x]
        pull[x] = scale * rho
        push[x] = scale * stiffness[x]
        inverse[x] = scale / rho
        damp[x] = 1.0 - step_length * sponge[x]
    loads[4].wait()

    sub = lax.broadcasted_iota(jnp.int32, (Y, Z), 0)
    lane = lax.broadcasted_iota(jnp.int32, (Y, Z), 1)
    first_y, last_y = sub == 0, sub == Y - 1
    first_z, last_z = lane == 0, lane == Z - 1

    def flux(v, joint, x, d):
        c = speed[d, x]
        q = [c * v[f] for f in range(F)]
        q[1 + d] = q[1 + d] + joint
        q[4] = q[4] + inverse[x] * v[1 + d]
        return q

    def joint_term(v, x):
        return pull[x] * v[0] + push[x] * v[4]

    def halo_copy(k, d, side):
        parts = pl.ds(0, F + 1 if k == 0 else F)
        if d == 0:
            src, dst = flux_x.at[k, (X - 1) * side, parts], halo_x.at[k, 1 - side, parts]
        elif d == 1:
            src, dst = send_y.at[k, side, parts], halo_y.at[k, 1 - side, parts]
        else:
            src, dst = send_z.at[k, side], halo_z.at[k, 1 - side]
        return pltpu.make_async_remote_copy(
            src_ref=src,
            dst_ref=dst,
            send_sem=halo_send_sem.at[k, d, side],
            recv_sem=halo_recv_sem.at[k, d, 1 - side],
            device_id=ups[d] if side else downs[d],
            device_id_type=MESH,
        )

    def send_halo(k, d):
        for side, has in ((1, has_up[d]), (0, has_down[d])):

            @pl.when(has)
            def _(side=side):
                halo_copy(k, d, side).start()

    def wait_halo(k, d):
        for side, has in ((1, has_down[d]), (0, has_up[d])):

            @pl.when(has)
            def _(side=side):
                halo_copy(k, d, side).wait_recv()

    def finish_halo(k, add):
        wait_halo(k, 1)
        wait_halo(k, 2)
        low_z, high_z = halo_z[k, 0], halo_z[k, 1]
        for f in range(F):
            low_y, high_y = halo_y[k, 0, f], halo_y[k, 1, f]
            for x in range(X):
                at = f * X + x
                delta = jnp.where(
                    last_y,
                    jnp.broadcast_to(high_y[x : x + 1], (Y, Z)),
                    jnp.where(first_y, -jnp.broadcast_to(low_y[x : x + 1], (Y, Z)), 0.0),
                )
                delta += jnp.where(
                    last_z,
                    jnp.broadcast_to(high_z[:, at : at + 1], (Y, Z)),
                    jnp.where(first_z, -jnp.broadcast_to(low_z[:, at : at + 1], (Y, Z)), 0.0),
                )
                add(f, x, delta)
        wait_halo(k, 0)
        for f in range(F):
            add(f, 0, -halo_x[k, 0, f])
            add(f, X - 1, halo_x[k, 1, f])

    def owner_of(i, j, k):
        return owner_ref[patch_ref[j, k, i]]

    def row_of(o):
        ox = lax.div(o, n_gy * n_gz)
        return lax.rem(ox, 2) * n_gy + lax.rem(lax.div(o, n_gz), n_gy)

    def cell_of(o):
        return lax.rem(o, n_gz) * n_plane + lax.div(o, 2 * n_gy * n_gz)

    row_index = lax.broadcasted_iota(jnp.int32, (TILE, Z), 0)

    def route_tables():
        owners = {}

        def owner(di, j, dk):
            if (di, j, dk) not in owners:
                i = jnp.clip(plane * 2 + di, 0, n_gx - 1)
                owners[di, j, dk] = owner_of(i, j, jnp.clip(gz + dk, 0, n_gz - 1))
            return owners[di, j, dk]

        lanes = lax.broadcasted_iota(jnp.int32, (1, n_row * TILE), 1)
        target = jnp.full((1, n_row * TILE), -1, jnp.int32)
        for t in range(n_row):
            di, j = t // n_gy, t % n_gy
            bricks = [(0, di, j, 0, None)]
            bricks.append((1, di + 1, j, 0, plane < n_plane - 1 if di == 1 else None))
            bricks.append((2, di - 1, j, 0, plane > 0 if di == 0 else None))
            if j < n_gy - 1:
                bricks.append((3, di, j + 1, 0, None))
            if j > 0:
                bricks.append((4, di, j - 1, 0, None))
            bricks.append((5, di, j, 1, has_up[2]))
            bricks.append((6, di, j, -1, has_down[2]))
            for r, bi, bj, bk, there in bricks:
                cell = cell_of(owner(bi, bj, bk))
                if there is not None:
                    cell = jnp.where(there, cell, -1)
                target = jnp.where(lanes == t * TILE + r, cell, target)
        choose[...] = (
            lax.broadcasted_iota(jnp.int32, (n_plane * n_gz, n_row * TILE), 0) == target
        ).astype(jnp.float32)
        to_row = jnp.full((TILE, Z), -1, jnp.int32)
        places = [(me, None)]
        for d in range(3):
            places += [(ups[d], has_up[d]), (downs[d], has_down[d])]
        for r, (place, there) in enumerate(places):
            row = row_of(owner_of(*place))
            if there is not None:
                row = jnp.where(there, row, -1)
            to_row = jnp.where(row_index == r, row, to_row)
        row_choice[...] = to_row
        spread_to = lax.broadcasted_iota(jnp.int32, (Z, Z), 1)
        spread[...] = (
            lax.broadcasted_iota(jnp.int32, (Z, Z), 0)
            == BZ * lax.rem(spread_to, BOXES) + lax.div(spread_to, BOXES)
        ).astype(jnp.float32)

    loads[5].wait()
    for side in range(2):
        flux_x[0, (X - 1) * side, F] = source[(X - 1) * side]

    for k in range(STAGES):
        for x in (0, X - 1):
            v = [fields[k, f, x] for f in range(F)]
            q = flux(v, joint_term(v, x), x, 0)
            for f in range(F):
                flux_x[k, x, f] = q[f]
        if k == 0:
            pl.semaphore_wait(barrier, expected)
        send_halo(k, 0)
        packs = [jnp.zeros((Y, Z), jnp.float32), jnp.zeros((Y, Z), jnp.float32)]
        for x in range(X):
            v = [fields[k, f, x] for f in range(F)]
            joint = joint_term(v, x)
            if 0 < x < X - 1:
                q = flux(v, joint, x, 0)
                for f in range(F):
                    flux_x[k, x, f] = q[f]
            q = flux(v, joint, x, 2)
            columns = q + [source[x]] if k == 0 else q
            for f, column in enumerate(columns):
                here = lane == f * X + x
                packs[0] = jnp.where(here, jnp.broadcast_to(column[:, 0:1], (Y, Z)), packs[0])
                packs[1] = jnp.where(here, jnp.broadcast_to(column[:, Z - 1 : Z], (Y, Z)), packs[1])
            for f in range(F):
                fields[k + 1, f, x] = (
                    damp[x] * v[f]
                    + jnp.where(last_z, 0.0, pltpu.roll(q[f], Z - 1, 1))
                    - jnp.where(first_z, 0.0, pltpu.roll(q[f], 1, 1))
                )
            q = flux(v, joint, x, 1)
            if k == 0:
                flux_y[k, F, pl.ds(x * Y, Y), :] = source[x]
            for f in range(F):
                flux_y[k, f, pl.ds(x * Y, Y), :] = q[f]
                fields[k + 1, f, x] += jnp.where(last_y, 0.0, pltpu.roll(q[f], Y - 1, 0)) - jnp.where(
                    first_y, 0.0, pltpu.roll(q[f], 1, 0)
                )
        for side in range(2):
            send_z[k, side] = packs[side]
        send_halo(k, 2)
        for f in range(F + 1 if k == 0 else F):
            for side in range(2):
                send_y[k, side, f] = flux_y[k, f, pl.ds((Y - 1) * side, X, stride=Y), :]
        send_halo(k, 1)
        for x in range(X):
            for f in range(F):
                if x == 0:
                    fields[k + 1, f, x] += flux_x[k, x + 1, f]
                elif x == X - 1:
                    fields[k + 1, f, x] -= flux_x[k, x - 1, f]
                else:
                    fields[k + 1, f, x] += flux_x[k, x + 1, f] - flux_x[k, x - 1, f]
        if k == 0:
            route_tables()
        if k < STAGES - 1:

            def add(f, x, delta):
                fields[k + 1, f, x] += delta

            finish_halo(k, add)

    sixth = 0.5 * third
    tiles = []
    for f in range(F):
        total = jnp.zeros((Y, Z), jnp.float32)
        for x in range(X):
            value = third * fields[0, f, x] + 0.5 * fields[1, f, x] + sixth * fields[STAGES, f, x]
            result[f, x] = value
            total += value * source[x]
        weighted = [
            total,
            -sixth * flux_x[STAGES - 1, X - 1, f] * halo_x[0, 1, F],
            sixth * flux_x[STAGES - 1, 0, f] * halo_x[0, 0, F],
            -sixth * send_y[STAGES - 1, 1, f] * halo_y[0, 1, F],
            sixth * send_y[STAGES - 1, 0, f] * halo_y[0, 0, F],
        ]
        tile = jnp.zeros((TILE, Z), jnp.float32)
        for r, product in enumerate(weighted):
            line = jnp.sum(product, axis=0, keepdims=True)
            tile = jnp.where(row_index == r, jnp.broadcast_to(line, (TILE, Z)), tile)
        tiles.append(tile)

    block = jnp.zeros((TILE, Z), jnp.float32)
    for f in range(F):
        tile = tiles[f]
        for shift in (1, 2, 4, 8):
            tile = tile + pltpu.roll(tile, Z - shift, 1)
        if f:
            tile = pltpu.roll(tile, f, 1)
        block = jnp.where(lax.rem(lane, BZ) == f, tile, block)
    for side, row, sign in ((1, 5, -sixth), (0, 6, sixth)):
        shape = halo_z[0, side]
        shapes = jnp.zeros((Y, Z), jnp.float32)
        for f in range(F):
            moved = pltpu.roll(shape, Z - (F - f) * X, 1)
            shapes = jnp.where(lax.div(lane, X) == f, moved, shapes)
        line = jnp.broadcast_to(
            jnp.sum(sign * send_z[STAGES - 1, side] * shapes, axis=0, keepdims=True), (TILE, Z)
        )
        for shift in (1, 2, 4):
            line = line + pltpu.roll(line, Z - shift, 1)
        box = 0 if side else Z - BZ
        for f in range(F):
            moved = pltpu.roll(line, (box + f - f * X) % Z, 1)
            block = jnp.where(jnp.logical_and(row_index == row, lane == box + f), moved, block)
    block = step_length * block

    to_row = row_choice[...]
    for t in range(n_row):
        row_send[t] = jnp.where(to_row == t, block, 0.0)

    def ring_copy(n, mine, device, src, dst, sems, r):
        t = lax.rem(mine + r, n)
        return pltpu.make_async_remote_copy(
            src_ref=src.at[t],
            dst_ref=dst.at[mine],
            send_sem=sems[0].at[r],
            recv_sem=sems[1].at[r],
            device_id=device(t),
            device_id_type=MESH,
        )

    row_copy = functools.partial(
        ring_copy, n_row, my_row, row_device, row_send, row_recv, (row_send_sem, row_recv_sem)
    )
    column_copy = functools.partial(
        ring_copy, n_gz, gz, column_device, column_send, column_recv, (column_send_sem, column_recv_sem)
    )
    plane_copy = functools.partial(
        ring_copy, n_plane, plane, plane_device, plane_send, plane_recv, (plane_send_sem, plane_recv_sem)
    )

    def far_first(n):
        return sorted(range(1, n), key=lambda r: -min(r, n - r))

    for r in far_first(n_row):
        row_copy(r).start()
    row_recv[my_row] = row_send[my_row]
    for r in range(1, n_row):
        row_copy(r).wait_recv()
    rows = row_recv[...].reshape(n_row * TILE, Z)
    cells = jnp.dot(
        choose[...], rows, preferred_element_type=jnp.float32, precision=lax.Precision.HIGHEST
    )
    for t in range(n_gz):
        column_send[t] = cells[t * n_plane : (t + 1) * n_plane]
    for r in far_first(n_gz):
        column_copy(r).start()
    column_recv[gz] = column_send[gz]

    def add_result(f, x, delta):
        result[f, x] += sixth * delta

    finish_halo(STAGES - 1, add_result)
    store = pltpu.make_async_copy(result, out_hbm, store_sem)
    store.start()

    for r in range(1, n_gz):
        column_copy(r).wait_recv()
    planes = column_recv[0]
    for t in range(1, n_gz):
        planes += column_recv[t]
    for t in range(n_plane):
        plane_send[t] = planes[t : t + 1]
    for r in far_first(n_plane):
        plane_copy(r).start()
    plane_recv[plane] = plane_send[plane]
    for k in range(STAGES):
        for d in range(3):
            for side, has in ((1, has_up[d]), (0, has_down[d])):

                @pl.when(has)
                def _(side=side, k=k, d=d):
                    halo_copy(k, d, side).wait_send()

    for r in range(1, n_row):
        row_copy(r).wait_send()
    for r in range(1, n_gz):
        column_copy(r).wait_send()
    store.wait()
    for r in range(1, n_plane):
        plane_copy(r).wait_recv()
    own = plane_recv[0]
    for t in range(1, n_plane):
        own += plane_recv[t]
    ordered = jnp.dot(
        own, spread[...], preferred_element_type=jnp.float32, precision=lax.Precision.HIGHEST
    )
    grad_ref[...] = ordered[:, : F * BOXES]
    for r in range(1, n_plane):
        plane_copy(r).wait_send()


def solution(mesh):
    sizes = tuple(mesh.shape[axis] for axis in AXES)
    n_row = 2 * sizes[1]
    n_plane = sizes[0] // 2
    n_gz = sizes[2]

    def body(
        terminal_adjoint,
        density,
        velocity,
        stiffness,
        sponge,
        source_shape,
        brick_level,
        brick_patch,
        patch_owner,
    ):
        f32 = jnp.float32
        smem = pl.BlockSpec(memory_space=pltpu.SMEM)
        hbm = pl.BlockSpec(memory_space=pl.ANY)
        return pl.pallas_call(
            functools.partial(kernel, sizes),
            out_shape=(
                jax.ShapeDtypeStruct((F, X, Y, Z), f32),
                jax.ShapeDtypeStruct((1, F * BOXES), f32),
            ),
            in_specs=[smem] * 3 + [hbm] * 6,
            out_specs=(hbm, pl.BlockSpec(memory_space=pltpu.VMEM)),
            scratch_shapes=[
                pltpu.VMEM((STAGES + 1, F, X, Y, Z), f32),
                pltpu.VMEM((X, Y, Z), f32),
                pltpu.VMEM((3, X, Y, Z), f32),
                pltpu.VMEM((X, Y, Z), f32),
                pltpu.VMEM((X, Y, Z), f32),
                pltpu.VMEM((X, Y, Z), f32),
                pltpu.VMEM((3, X, Y, Z), f32),
                pltpu.VMEM((X, Y, Z), f32),
                pltpu.VMEM((X, Y, Z), f32),
                pltpu.VMEM((X, Y, Z), f32),
                pltpu.VMEM((X, Y, Z), f32),
                pltpu.VMEM((STAGES, X, F + 1, Y, Z), f32),
                pltpu.VMEM((STAGES, F + 1, X * Y, Z), f32),
                pltpu.VMEM((STAGES, 2, F + 1, X, Z), f32),
                pltpu.VMEM((STAGES, 2, Y, Z), f32),
                pltpu.VMEM((STAGES, 2, F + 1, Y, Z), f32),
                pltpu.VMEM((STAGES, 2, F + 1, X, Z), f32),
                pltpu.VMEM((STAGES, 2, Y, Z), f32),
                pltpu.VMEM((F, X, Y, Z), f32),
                pltpu.VMEM((n_plane * n_gz, n_row * TILE), f32),
                pltpu.VMEM((TILE, Z), jnp.int32),
                pltpu.VMEM((Z, Z), f32),
                pltpu.VMEM((n_row, TILE, Z), f32),
                pltpu.VMEM((n_row, TILE, Z), f32),
                pltpu.VMEM((n_gz, n_plane, Z), f32),
                pltpu.VMEM((n_gz, n_plane, Z), f32),
                pltpu.VMEM((n_plane, 1, Z), f32),
                pltpu.VMEM((n_plane, 1, Z), f32),
                pltpu.SemaphoreType.DMA((6,)),
                pltpu.SemaphoreType.DMA,
                pltpu.SemaphoreType.DMA((STAGES, 3, 2)),
                pltpu.SemaphoreType.DMA((STAGES, 3, 2)),
                pltpu.SemaphoreType.DMA((n_row,)),
                pltpu.SemaphoreType.DMA((n_row,)),
                pltpu.SemaphoreType.DMA((n_gz,)),
                pltpu.SemaphoreType.DMA((n_gz,)),
                pltpu.SemaphoreType.DMA((n_plane,)),
                pltpu.SemaphoreType.DMA((n_plane,)),
            ],
            compiler_params=pltpu.CompilerParams(collective_id=0, has_side_effects=True),
        )(
            jnp.transpose(brick_level, (1, 2, 0)),
            jnp.transpose(brick_patch, (1, 2, 0)),
            patch_owner,
            terminal_adjoint,
            density,
            velocity,
            stiffness,
            sponge,
            source_shape,
        )

    in_specs = (
        P(None, "gx", "gy", "gz"),
        P("gx", "gy", "gz"),
        P(None, "gx", "gy", "gz"),
        P("gx", "gy", "gz"),
        P("gx", "gy", "gz"),
        P("gx", "gy", "gz"),
        P(),
        P(),
        P(),
    )
    out_specs = (P(None, "gx", "gy", "gz"), P(AXES, None))
    return jax.shard_map(body, mesh=mesh, in_specs=in_specs, out_specs=out_specs, check_vma=False)
```

```python
import functools

import jax
import jax.numpy as jnp
from jax import lax
from jax.experimental import pallas as pl
from jax.experimental.pallas import tpu as pltpu
from jax.sharding import PartitionSpec as P

MESH = pl.DeviceIdType.MESH
F = 5
X = 8
Y = 8
Z = 128
BZ = 16
BOXES = Z // BZ
TILE = 8
STAGES = 3
step_length = 0.14
third = 1.0 / 3.0
AXES = ("gx", "gy", "gz")


def kernel(
    sizes,
    level_hbm,
    patch_hbm,
    owner_hbm,
    adjoint_hbm,
    density_hbm,
    velocity_hbm,
    stiffness_hbm,
    sponge_hbm,
    source_hbm,
    result,
    grad_ref,
    level_ref,
    patch_ref,
    owner_ref,
    fields,
    density,
    velocity,
    stiffness,
    sponge,
    source,
    speed,
    pull,
    push,
    inverse,
    damp,
    flux_x,
    flux_y,
    send_y,
    send_z,
    halo_x,
    halo_y,
    halo_z,
    choose,
    row_choice,
    spread,
    row_send,
    row_recv,
    column_send,
    column_recv,
    plane_send,
    plane_recv,
    load_sem,
    halo_send_sem,
    halo_recv_sem,
    row_send_sem,
    row_recv_sem,
    column_send_sem,
    column_recv_sem,
    plane_send_sem,
    plane_recv_sem,
    token_sem,
):
    n_gx, n_gy, n_gz = sizes
    gx, gy, gz = (lax.axis_index(axis) for axis in AXES)
    half = lax.rem(gx, 2)
    plane = lax.div(gx, 2)
    n_plane = n_gx // 2
    n_row = 2 * n_gy
    my_row = half * n_gy + gy

    def row_device(t):
        return (plane * 2 + lax.div(t, n_gy), lax.rem(t, n_gy), gz)

    def column_device(t):
        return (gx, gy, t)

    def plane_device(t):
        return (t * 2 + half, gy, gz)

    barrier = pltpu.get_barrier_semaphore()
    me = (gx, gy, gz)
    ups, downs, has_up, has_down = [], [], [], []
    for d in range(3):
        up, down = list(me), list(me)
        up[d] = jnp.minimum(me[d] + 1, sizes[d] - 1)
        down[d] = jnp.maximum(me[d] - 1, 0)
        ups.append(tuple(up))
        downs.append(tuple(down))
        has_up.append(me[d] < sizes[d] - 1)
        has_down.append(me[d] > 0)

    def greet(to):
        pl.semaphore_signal(barrier, inc=1, device_id=to, device_id_type=MESH)

    cross_up = jnp.logical_and(half == 1, has_up[0])
    cross_down = jnp.logical_and(half == 0, has_down[0])
    for has, to in ((cross_up, ups[0]), (cross_down, downs[0])):

        @pl.when(has)
        def _(to=to):
            greet(to)

    rings = (
        (n_row, my_row, row_device, (n_row // 2, 1, n_row - 1)),
        (n_gz, gz, column_device, (1, n_gz - 1)),
        (n_plane, plane, plane_device, (1, n_plane - 1)),
    )
    for n, mine, device, near in rings:
        for r in near:
            greet(device(lax.rem(mine + r, n)))
    expected = (
        jnp.int32(sum(len(near) for _, _, _, near in rings))
        + jnp.where(cross_up, 1, 0)
        + jnp.where(cross_down, 1, 0)
    )

    def send_tokens(level):
        for ring, (n, mine, device, _) in enumerate(rings):
            for r in (level, n - level):
                pl.semaphore_signal(
                    token_sem.at[ring, level - 1],
                    inc=1,
                    device_id=device(lax.rem(mine + r, n)),
                    device_id_type=MESH,
                )

    def wait_tokens(level):
        for ring in range(len(rings)):
            pl.semaphore_wait(token_sem.at[ring, level - 1], 2)

    loads = []
    for i, (src, dst) in enumerate(
        (
            (density_hbm, density),
            (velocity_hbm, velocity),
            (stiffness_hbm, stiffness),
            (sponge_hbm, sponge),
            (adjoint_hbm, fields.at[0]),
            (source_hbm, source),
            (level_hbm, level_ref),
            (patch_hbm, patch_ref),
            (owner_hbm, owner_ref),
        )
    ):
        copy = pltpu.make_async_copy(src, dst, load_sem.at[i])
        copy.start()
        loads.append(copy)

    for d, halo in enumerate((halo_x, halo_y, halo_z)):
        for side, has in ((0, has_down[d]), (1, has_up[d])):

            @pl.when(jnp.logical_not(has))
            def _(halo=halo, side=side):
                for k in range(STAGES):
                    halo[k, side] = jnp.zeros(halo.shape[2:], jnp.float32)

    loads[6].wait()
    level = level_ref[gy, gz, gx]
    scale = 0.5 * step_length * lax.shift_left(jnp.int32(1), level).astype(jnp.float32)
    for copy in loads[:4]:
        copy.wait()
    for x in range(X):
        rho = density[x]
        speed[:, x] = scale * velocity[:, x]
        pull[x] = scale * rho
        push[x] = scale * stiffness[x]
        inverse[x] = scale / rho
        damp[x] = 1.0 - step_length * sponge[x]
    loads[4].wait()

    sub = lax.broadcasted_iota(jnp.int32, (Y, Z), 0)
    lane = lax.broadcasted_iota(jnp.int32, (Y, Z), 1)
    first_y, last_y = sub == 0, sub == Y - 1
    first_z, last_z = lane == 0, lane == Z - 1

    def flux(v, joint, x, d):
        c = speed[d, x]
        q = [c * v[f] for f in range(F)]
        q[1 + d] = q[1 + d] + joint
        q[4] = q[4] + inverse[x] * v[1 + d]
        return q

    def joint_term(v, x):
        return pull[x] * v[0] + push[x] * v[4]

    def halo_copy(k, d, side):
        parts = pl.ds(0, F + 1 if k == 0 else F)
        if d == 0:
            src, dst = flux_x.at[k, (X - 1) * side, parts], halo_x.at[k, 1 - side, parts]
        elif d == 1:
            src, dst = send_y.at[k, side, parts], halo_y.at[k, 1 - side, parts]
        else:
            src, dst = send_z.at[k, side], halo_z.at[k, 1 - side]
        return pltpu.make_async_remote_copy(
            src_ref=src,
            dst_ref=dst,
            send_sem=halo_send_sem.at[k, d, side],
            recv_sem=halo_recv_sem.at[k, d, 1 - side],
            device_id=ups[d] if side else downs[d],
            device_id_type=MESH,
        )

    def send_halo(k, d):
        for side, has in ((1, has_up[d]), (0, has_down[d])):

            @pl.when(has)
            def _(side=side):
                halo_copy(k, d, side).start()

    def wait_halo(k, d):
        for side, has in ((1, has_down[d]), (0, has_up[d])):

            @pl.when(has)
            def _(side=side):
                halo_copy(k, d, side).wait_recv()

    def finish_halo(k, add):
        wait_halo(k, 1)
        wait_halo(k, 2)
        low_z, high_z = halo_z[k, 0], halo_z[k, 1]
        for f in range(F):
            low_y, high_y = halo_y[k, 0, f], halo_y[k, 1, f]
            for x in range(X):
                at = f * X + x
                delta = jnp.where(
                    last_y,
                    jnp.broadcast_to(high_y[x : x + 1], (Y, Z)),
                    jnp.where(first_y, -jnp.broadcast_to(low_y[x : x + 1], (Y, Z)), 0.0),
                )
                delta += jnp.where(
                    last_z,
                    jnp.broadcast_to(high_z[:, at : at + 1], (Y, Z)),
                    jnp.where(first_z, -jnp.broadcast_to(low_z[:, at : at + 1], (Y, Z)), 0.0),
                )
                add(f, x, delta)
        wait_halo(k, 0)
        for f in range(F):
            add(f, 0, -halo_x[k, 0, f])
            add(f, X - 1, halo_x[k, 1, f])

    def owner_of(i, j, k):
        return owner_ref[patch_ref[j, k, i]]

    def row_of(o):
        ox = lax.div(o, n_gy * n_gz)
        return lax.rem(ox, 2) * n_gy + lax.rem(lax.div(o, n_gz), n_gy)

    def cell_of(o):
        return lax.rem(o, n_gz) * n_plane + lax.div(o, 2 * n_gy * n_gz)

    row_index = lax.broadcasted_iota(jnp.int32, (TILE, Z), 0)

    def route_tables():
        owners = {}

        def owner(di, j, dk):
            if (di, j, dk) not in owners:
                i = jnp.clip(plane * 2 + di, 0, n_gx - 1)
                owners[di, j, dk] = owner_of(i, j, jnp.clip(gz + dk, 0, n_gz - 1))
            return owners[di, j, dk]

        lanes = lax.broadcasted_iota(jnp.int32, (1, n_row * TILE), 1)
        target = jnp.full((1, n_row * TILE), -1, jnp.int32)
        for t in range(n_row):
            di, j = t // n_gy, t % n_gy
            bricks = [(0, di, j, 0, None)]
            bricks.append((1, di + 1, j, 0, plane < n_plane - 1 if di == 1 else None))
            bricks.append((2, di - 1, j, 0, plane > 0 if di == 0 else None))
            if j < n_gy - 1:
                bricks.append((3, di, j + 1, 0, None))
            if j > 0:
                bricks.append((4, di, j - 1, 0, None))
            bricks.append((5, di, j, 1, has_up[2]))
            bricks.append((6, di, j, -1, has_down[2]))
            for r, bi, bj, bk, there in bricks:
                cell = cell_of(owner(bi, bj, bk))
                if there is not None:
                    cell = jnp.where(there, cell, -1)
                target = jnp.where(lanes == t * TILE + r, cell, target)
        choose[...] = (
            lax.broadcasted_iota(jnp.int32, (n_plane * n_gz, n_row * TILE), 0) == target
        ).astype(jnp.float32)
        to_row = jnp.full((TILE, Z), -1, jnp.int32)
        places = [(me, None)]
        for d in range(3):
            places += [(ups[d], has_up[d]), (downs[d], has_down[d])]
        for r, (place, there) in enumerate(places):
            row = row_of(owner_of(*place))
            if there is not None:
                row = jnp.where(there, row, -1)
            to_row = jnp.where(row_index == r, row, to_row)
        row_choice[...] = to_row
        spread_to = lax.broadcasted_iota(jnp.int32, (Z, Z), 1)
        spread[...] = (
            lax.broadcasted_iota(jnp.int32, (Z, Z), 0)
            == BZ * lax.rem(spread_to, BOXES) + lax.div(spread_to, BOXES)
        ).astype(jnp.float32)

    loads[5].wait()
    for side in range(2):
        flux_x[0, (X - 1) * side, F] = source[(X - 1) * side]

    for k in range(STAGES):
        for x in (0, X - 1):
            v = [fields[k, f, x] for f in range(F)]
            q = flux(v, joint_term(v, x), x, 0)
            for f in range(F):
                flux_x[k, x, f] = q[f]
        if k == 0:
            pl.semaphore_wait(barrier, expected)
        send_halo(k, 0)
        packs = [jnp.zeros((Y, Z), jnp.float32), jnp.zeros((Y, Z), jnp.float32)]
        for x in range(X):
            v = [fields[k, f, x] for f in range(F)]
            joint = joint_term(v, x)
            if 0 < x < X - 1:
                q = flux(v, joint, x, 0)
                for f in range(F):
                    flux_x[k, x, f] = q[f]
            q = flux(v, joint, x, 2)
            columns = q + [source[x]] if k == 0 else q
            for f, column in enumerate(columns):
                here = lane == f * X + x
                packs[0] = jnp.where(here, jnp.broadcast_to(column[:, 0:1], (Y, Z)), packs[0])
                packs[1] = jnp.where(here, jnp.broadcast_to(column[:, Z - 1 : Z], (Y, Z)), packs[1])
            for f in range(F):
                fields[k + 1, f, x] = (
                    damp[x] * v[f]
                    + jnp.where(last_z, 0.0, pltpu.roll(q[f], Z - 1, 1))
                    - jnp.where(first_z, 0.0, pltpu.roll(q[f], 1, 1))
                )
            q = flux(v, joint, x, 1)
            if k == 0:
                flux_y[k, F, pl.ds(x * Y, Y), :] = source[x]
            for f in range(F):
                flux_y[k, f, pl.ds(x * Y, Y), :] = q[f]
                fields[k + 1, f, x] += jnp.where(last_y, 0.0, pltpu.roll(q[f], Y - 1, 0)) - jnp.where(
                    first_y, 0.0, pltpu.roll(q[f], 1, 0)
                )
        for side in range(2):
            send_z[k, side] = packs[side]
        send_halo(k, 2)
        for f in range(F + 1 if k == 0 else F):
            for side in range(2):
                send_y[k, side, f] = flux_y[k, f, pl.ds((Y - 1) * side, X, stride=Y), :]
        send_halo(k, 1)
        for x in range(X):
            for f in range(F):
                if x == 0:
                    fields[k + 1, f, x] += flux_x[k, x + 1, f]
                elif x == X - 1:
                    fields[k + 1, f, x] -= flux_x[k, x - 1, f]
                else:
                    fields[k + 1, f, x] += flux_x[k, x + 1, f] - flux_x[k, x - 1, f]
        if k == 0:
            send_tokens(1)
            loads[7].wait()
            loads[8].wait()
            route_tables()
            wait_tokens(1)
            send_tokens(2)
        if k < STAGES - 1:

            def add(f, x, delta):
                fields[k + 1, f, x] += delta

            finish_halo(k, add)

    wait_tokens(2)
    sixth = 0.5 * third
    tiles = []
    for f in range(F):
        total = jnp.zeros((Y, Z), jnp.float32)
        for x in range(X):
            value = third * fields[0, f, x] + 0.5 * fields[1, f, x] + sixth * fields[STAGES, f, x]
            result[f, x] = value
            total += value * source[x]
        weighted = [
            total,
            -sixth * flux_x[STAGES - 1, X - 1, f] * halo_x[0, 1, F],
            sixth * flux_x[STAGES - 1, 0, f] * halo_x[0, 0, F],
            -sixth * send_y[STAGES - 1, 1, f] * halo_y[0, 1, F],
            sixth * send_y[STAGES - 1, 0, f] * halo_y[0, 0, F],
        ]
        tile = jnp.zeros((TILE, Z), jnp.float32)
        for r, product in enumerate(weighted):
            line = jnp.sum(product, axis=0, keepdims=True)
            tile = jnp.where(row_index == r, jnp.broadcast_to(line, (TILE, Z)), tile)
        tiles.append(tile)

    block = jnp.zeros((TILE, Z), jnp.float32)
    for f in range(F):
        tile = tiles[f]
        for shift in (1, 2, 4, 8):
            tile = tile + pltpu.roll(tile, Z - shift, 1)
        if f:
            tile = pltpu.roll(tile, f, 1)
        block = jnp.where(lax.rem(lane, BZ) == f, tile, block)
    for side, row, sign in ((1, 5, -sixth), (0, 6, sixth)):
        shape = halo_z[0, side]
        shapes = jnp.zeros((Y, Z), jnp.float32)
        for f in range(F):
            moved = pltpu.roll(shape, Z - (F - f) * X, 1)
            shapes = jnp.where(lax.div(lane, X) == f, moved, shapes)
        line = jnp.broadcast_to(
            jnp.sum(sign * send_z[STAGES - 1, side] * shapes, axis=0, keepdims=True), (TILE, Z)
        )
        for shift in (1, 2, 4):
            line = line + pltpu.roll(line, Z - shift, 1)
        box = 0 if side else Z - BZ
        for f in range(F):
            moved = pltpu.roll(line, (box + f - f * X) % Z, 1)
            block = jnp.where(jnp.logical_and(row_index == row, lane == box + f), moved, block)
    block = step_length * block

    to_row = row_choice[...]
    for t in range(n_row):
        row_send[t] = jnp.where(to_row == t, block, 0.0)

    def ring_copy(n, mine, device, src, dst, sems, r):
        t = lax.rem(mine + r, n)
        return pltpu.make_async_remote_copy(
            src_ref=src.at[t],
            dst_ref=dst.at[mine],
            send_sem=sems[0].at[r],
            recv_sem=sems[1].at[r],
            device_id=device(t),
            device_id_type=MESH,
        )

    row_copy = functools.partial(
        ring_copy, n_row, my_row, row_device, row_send, row_recv, (row_send_sem, row_recv_sem)
    )
    column_copy = functools.partial(
        ring_copy, n_gz, gz, column_device, column_send, column_recv, (column_send_sem, column_recv_sem)
    )
    plane_copy = functools.partial(
        ring_copy, n_plane, plane, plane_device, plane_send, plane_recv, (plane_send_sem, plane_recv_sem)
    )

    def far_first(n):
        return sorted(range(1, n), key=lambda r: -min(r, n - r))

    for r in far_first(n_row):
        row_copy(r).start()
    row_recv[my_row] = row_send[my_row]
    for r in range(1, n_row):
        row_copy(r).wait_recv()
    rows = row_recv[...].reshape(n_row * TILE, Z)
    cells = jnp.dot(
        choose[...], rows, preferred_element_type=jnp.float32, precision=lax.Precision.HIGHEST
    )
    for t in range(n_gz):
        column_send[t] = cells[t * n_plane : (t + 1) * n_plane]
    for r in far_first(n_gz):
        column_copy(r).start()
    column_recv[gz] = column_send[gz]

    def add_result(f, x, delta):
        result[f, x] += sixth * delta

    finish_halo(STAGES - 1, add_result)

    for r in range(1, n_gz):
        column_copy(r).wait_recv()
    planes = column_recv[0]
    for t in range(1, n_gz):
        planes += column_recv[t]
    for t in range(n_plane):
        plane_send[t] = planes[t : t + 1]
    for r in far_first(n_plane):
        plane_copy(r).start()
    plane_recv[plane] = plane_send[plane]
    for k in range(STAGES):
        for d in range(3):
            for side, has in ((1, has_up[d]), (0, has_down[d])):

                @pl.when(has)
                def _(side=side, k=k, d=d):
                    halo_copy(k, d, side).wait_send()

    for r in range(1, n_row):
        row_copy(r).wait_send()
    for r in range(1, n_gz):
        column_copy(r).wait_send()
    for r in range(1, n_plane):
        plane_copy(r).wait_recv()
    own = plane_recv[0]
    for t in range(1, n_plane):
        own += plane_recv[t]
    ordered = jnp.dot(
        own, spread[...], preferred_element_type=jnp.float32, precision=lax.Precision.HIGHEST
    )
    grad_ref[...] = ordered[:, : F * BOXES]
    for r in range(1, n_plane):
        plane_copy(r).wait_send()


def solution(mesh):
    sizes = tuple(mesh.shape[axis] for axis in AXES)
    n_row = 2 * sizes[1]
    n_plane = sizes[0] // 2
    n_gz = sizes[2]

    def body(
        terminal_adjoint,
        density,
        velocity,
        stiffness,
        sponge,
        source_shape,
        brick_level,
        brick_patch,
        patch_owner,
    ):
        f32 = jnp.float32
        hbm = pl.BlockSpec(memory_space=pl.ANY)
        return pl.pallas_call(
            functools.partial(kernel, sizes),
            out_shape=(
                pltpu.VMEM((F, X, Y, Z), f32),
                pltpu.VMEM((1, F * BOXES), f32),
            ),
            in_specs=[hbm] * 9,
            out_specs=(pl.BlockSpec(memory_space=pltpu.VMEM),) * 2,
            scratch_shapes=[
                pltpu.SMEM((sizes[1], sizes[2], sizes[0]), jnp.int32),
                pltpu.SMEM((sizes[1], sizes[2], sizes[0]), jnp.int32),
                pltpu.SMEM((sizes[0] * sizes[1] * sizes[2],), jnp.int32),
                pltpu.VMEM((STAGES + 1, F, X, Y, Z), f32),
                pltpu.VMEM((X, Y, Z), f32),
                pltpu.VMEM((3, X, Y, Z), f32),
                pltpu.VMEM((X, Y, Z), f32),
                pltpu.VMEM((X, Y, Z), f32),
                pltpu.VMEM((X, Y, Z), f32),
                pltpu.VMEM((3, X, Y, Z), f32),
                pltpu.VMEM((X, Y, Z), f32),
                pltpu.VMEM((X, Y, Z), f32),
                pltpu.VMEM((X, Y, Z), f32),
                pltpu.VMEM((X, Y, Z), f32),
                pltpu.VMEM((STAGES, X, F + 1, Y, Z), f32),
                pltpu.VMEM((STAGES, F + 1, X * Y, Z), f32),
                pltpu.VMEM((STAGES, 2, F + 1, X, Z), f32),
                pltpu.VMEM((STAGES, 2, Y, Z), f32),
                pltpu.VMEM((STAGES, 2, F + 1, Y, Z), f32),
                pltpu.VMEM((STAGES, 2, F + 1, X, Z), f32),
                pltpu.VMEM((STAGES, 2, Y, Z), f32),
                pltpu.VMEM((n_plane * n_gz, n_row * TILE), f32),
                pltpu.VMEM((TILE, Z), jnp.int32),
                pltpu.VMEM((Z, Z), f32),
                pltpu.VMEM((n_row, TILE, Z), f32),
                pltpu.VMEM((n_row, TILE, Z), f32),
                pltpu.VMEM((n_gz, n_plane, Z), f32),
                pltpu.VMEM((n_gz, n_plane, Z), f32),
                pltpu.VMEM((n_plane, 1, Z), f32),
                pltpu.VMEM((n_plane, 1, Z), f32),
                pltpu.SemaphoreType.DMA((9,)),
                pltpu.SemaphoreType.DMA((STAGES, 3, 2)),
                pltpu.SemaphoreType.DMA((STAGES, 3, 2)),
                pltpu.SemaphoreType.DMA((n_row,)),
                pltpu.SemaphoreType.DMA((n_row,)),
                pltpu.SemaphoreType.DMA((n_gz,)),
                pltpu.SemaphoreType.DMA((n_gz,)),
                pltpu.SemaphoreType.DMA((n_plane,)),
                pltpu.SemaphoreType.DMA((n_plane,)),
                pltpu.SemaphoreType.REGULAR((3, 2)),
            ],
            compiler_params=pltpu.CompilerParams(collective_id=0, has_side_effects=True),
        )(
            jnp.transpose(brick_level, (1, 2, 0)),
            jnp.transpose(brick_patch, (1, 2, 0)),
            patch_owner,
            terminal_adjoint,
            density,
            velocity,
            stiffness,
            sponge,
            source_shape,
        )

    in_specs = (
        P(None, "gx", "gy", "gz"),
        P("gx", "gy", "gz"),
        P(None, "gx", "gy", "gz"),
        P("gx", "gy", "gz"),
        P("gx", "gy", "gz"),
        P("gx", "gy", "gz"),
        P(),
        P(),
        P(),
    )
    out_specs = (P(None, "gx", "gy", "gz"), P(AXES, None))
    return jax.shard_map(body, mesh=mesh, in_specs=in_specs, out_specs=out_specs, check_vma=False)
```

```python
import functools

import jax
import jax.numpy as jnp
from jax import lax
from jax.experimental import pallas as pl
from jax.experimental.pallas import tpu as pltpu
from jax.sharding import PartitionSpec as P

MESH = pl.DeviceIdType.MESH
F = 5
X = 8
Y = 8
Z = 128
BZ = 16
BOXES = Z // BZ
TILE = 8
ROWS = TILE // 2
LAYERS = 5
STAGES = 3
step_length = 0.14
third = 1.0 / 3.0
AXES = ("gx", "gy", "gz")


def kernel(
    sizes,
    level_hbm,
    patch_hbm,
    owner_hbm,
    adjoint_hbm,
    density_hbm,
    velocity_hbm,
    stiffness_hbm,
    sponge_hbm,
    source_hbm,
    result,
    grad_ref,
    level_ref,
    patch_ref,
    owner_ref,
    fields,
    density,
    velocity,
    stiffness,
    sponge,
    source,
    speed,
    pull,
    push,
    inverse,
    damp,
    flux_x,
    flux_y,
    send_y,
    send_z,
    halo_x,
    halo_y,
    halo_z,
    send_x,
    layers,
    halo_layers,
    choose,
    row_choice,
    spread,
    row_send,
    row_recv,
    cell_send,
    cell_recv,
    load_sem,
    halo_send_sem,
    halo_recv_sem,
    layer_send_sem,
    layer_recv_sem,
    row_send_sem,
    row_recv_sem,
    cell_send_sem,
    cell_recv_sem,
    token_sem,
    line_sem,
):
    n_gx, n_gy, n_gz = sizes
    gx, gy, gz = (lax.axis_index(axis) for axis in AXES)
    half = lax.rem(gx, 2)
    plane = lax.div(gx, 2)
    n_plane = n_gx // 2
    n_row = 2 * n_gy
    my_row = half * n_gy + gy
    my_cell = gz * n_plane + plane

    def row_device(t):
        return (plane * 2 + lax.div(t, n_gy), lax.rem(t, n_gy), gz)

    def column_device(t):
        return (gx, gy, t)

    def plane_device(t):
        return (t * 2 + half, gy, gz)

    def cell_device(dz, dy):
        return (lax.rem(plane + dz, n_plane) * 2 + half, gy, lax.rem(gz + dy, n_gz))

    def cell_row(dz, dy):
        return lax.rem(gz + dy, n_gz) * n_plane + lax.rem(plane + dz, n_plane)

    barrier = pltpu.get_barrier_semaphore()
    me = (gx, gy, gz)
    ups, downs, has_up, has_down = [], [], [], []
    for d in range(3):
        up, down = list(me), list(me)
        up[d] = jnp.minimum(me[d] + 1, sizes[d] - 1)
        down[d] = jnp.maximum(me[d] - 1, 0)
        ups.append(tuple(up))
        downs.append(tuple(down))
        has_up.append(me[d] < sizes[d] - 1)
        has_down.append(me[d] > 0)

    loads = []
    for i, (src, dst) in enumerate(
        (
            (density_hbm, density),
            (velocity_hbm, velocity),
            (stiffness_hbm, stiffness),
            (sponge_hbm, sponge),
            (adjoint_hbm, fields.at[0]),
            (source_hbm, source),
            (level_hbm, level_ref),
            (patch_hbm, patch_ref),
            (owner_hbm, owner_ref),
        )
    ):
        copy = pltpu.make_async_copy(src, dst, load_sem.at[i])
        copy.start()
        loads.append(copy)

    def greet(to):
        pl.semaphore_signal(barrier, inc=1, device_id=to, device_id_type=MESH)

    cross_up = jnp.logical_and(half == 1, has_up[0])
    cross_down = jnp.logical_and(half == 0, has_down[0])
    for has, to in ((cross_up, ups[0]), (cross_down, downs[0])):

        @pl.when(has)
        def _(to=to):
            greet(to)

    rings = (
        (n_row, my_row, row_device, (n_row // 2, 1, n_row - 1)),
        (n_gz, gz, column_device, (1, n_gz - 1)),
    )
    for n, mine, device, near in rings:
        for r in near:
            greet(device(lax.rem(mine + r, n)))

    def planes_at(step):
        up, down = plane + step, plane - step
        return (
            (up < n_plane, plane_device(jnp.minimum(up, n_plane - 1))),
            (down >= 0, plane_device(jnp.maximum(down, 0))),
        )

    def line_count(step):
        return sum(jnp.where(has, 1, 0) for has, _ in planes_at(step))

    for has, to in planes_at(1):

        @pl.when(has)
        def _(to=to):
            greet(to)

    expected = (
        jnp.int32(sum(len(near) for _, _, _, near in rings))
        + line_count(1)
        + jnp.where(cross_up, 1, 0)
        + jnp.where(cross_down, 1, 0)
    )

    def send_tokens(level):
        for ring, (n, mine, device, _) in enumerate(rings):
            for r in (level, n - level):
                pl.semaphore_signal(
                    token_sem.at[ring, level - 1],
                    inc=1,
                    device_id=device(lax.rem(mine + r, n)),
                    device_id_type=MESH,
                )

    def wait_tokens(level):
        for ring in range(len(rings)):
            pl.semaphore_wait(token_sem.at[ring, level - 1], 2)

    def send_line(level):
        for has, to in planes_at(1 << level):

            @pl.when(has)
            def _(to=to):
                pl.semaphore_signal(
                    line_sem.at[level], inc=1, device_id=to, device_id_type=MESH
                )

    def wait_line(level):
        pl.semaphore_wait(line_sem.at[level], line_count(1 << level))

    for d, halo in enumerate((halo_x, halo_y, halo_z)):
        for side, has in ((0, has_down[d]), (1, has_up[d])):

            @pl.when(jnp.logical_not(has))
            def _(halo=halo, side=side):
                for k in range(STAGES):
                    halo[k, side] = jnp.zeros(halo.shape[2:], jnp.float32)
                if halo is halo_x:
                    halo_layers[side] = jnp.zeros(halo_layers.shape[1:], jnp.float32)

    loads[6].wait()
    level = level_ref[gy, gz, gx]
    scale = 0.5 * step_length * lax.shift_left(jnp.int32(1), level).astype(jnp.float32)
    for copy in loads[:4]:
        copy.wait()
    for x in range(X):
        rho = density[x]
        speed[:, x] = scale * velocity[:, x]
        pull[x] = scale * rho
        push[x] = scale * stiffness[x]
        inverse[x] = scale / rho
        damp[x] = 1.0 - step_length * sponge[x]
    loads[4].wait()

    sub = lax.broadcasted_iota(jnp.int32, (Y, Z), 0)
    lane = lax.broadcasted_iota(jnp.int32, (Y, Z), 1)
    first_y, last_y = sub == 0, sub == Y - 1
    first_z, last_z = lane == 0, lane == Z - 1

    def flux(v, joint, x, d):
        c = speed[d, x]
        q = [c * v[f] for f in range(F)]
        q[1 + d] = q[1 + d] + joint
        q[4] = q[4] + inverse[x] * v[1 + d]
        return q

    def joint_term(v, x):
        return pull[x] * v[0] + push[x] * v[4]

    def halo_copy(k, d, side):
        parts = pl.ds(0, F + 1 if k == 0 else F)
        if d == 0:
            src = send_x.at[side] if k == 1 else flux_x.at[k, (X - 1) * side]
            dst = halo_x.at[k, 1 - side]
        elif d == 1:
            src, dst = send_y.at[k, side, parts], halo_y.at[k, 1 - side, parts]
        else:
            src, dst = send_z.at[k, side], halo_z.at[k, 1 - side]
        return pltpu.make_async_remote_copy(
            src_ref=src,
            dst_ref=dst,
            send_sem=halo_send_sem.at[k, d, side],
            recv_sem=halo_recv_sem.at[k, d, 1 - side],
            device_id=ups[d] if side else downs[d],
            device_id_type=MESH,
        )

    def send_halo(k, d):
        for side, has in ((1, has_up[d]), (0, has_down[d])):

            @pl.when(has)
            def _(side=side):
                halo_copy(k, d, side).start()

    def wait_halo(k, d):
        for side, has in ((1, has_down[d]), (0, has_up[d])):

            @pl.when(has)
            def _(side=side):
                halo_copy(k, d, side).wait_recv()

    def layer_copy(side):
        return pltpu.make_async_remote_copy(
            src_ref=layers.at[side],
            dst_ref=halo_layers.at[1 - side],
            send_sem=layer_send_sem.at[side],
            recv_sem=layer_recv_sem.at[1 - side],
            device_id=ups[0] if side else downs[0],
            device_id_type=MESH,
        )

    def each_side(act, up_first):
        for side in (1, 0):
            has = (has_up if (side == 1) == up_first else has_down)[0]

            @pl.when(has)
            def _(side=side):
                act(layer_copy(side))

    def send_outermost():
        for side in range(2):
            for f in range(F):
                send_x[side, f] = fields[1, f, (X - 1) * side]
        send_halo(1, 0)

    def neighbour_flux(side):
        at, sign = ((0, 1.0), (X - 1, -1.0))[side]
        v = [halo_x[1, side, f] + sign * flux_x[0, at, f] for f in range(F)]
        q = [halo_layers[side, 1] * v[f] for f in range(F)]
        q[1] = q[1] + (halo_layers[side, 2] * v[0] + halo_layers[side, 3] * v[4])
        q[4] = q[4] + halo_layers[side, 4] * v[1]
        return q

    def finish_halo(k, add, between=None):
        wait_halo(k, 1)
        wait_halo(k, 2)
        low_z, high_z = halo_z[k, 0], halo_z[k, 1]
        for x in (0, X - 1, *range(1, X - 1)):
            if k == 0 and x == 1:
                send_outermost()
            for f in range(F):
                low_y, high_y = halo_y[k, 0, f], halo_y[k, 1, f]
                at = f * X + x
                delta = jnp.where(
                    last_y,
                    jnp.broadcast_to(high_y[x : x + 1], (Y, Z)),
                    jnp.where(first_y, -jnp.broadcast_to(low_y[x : x + 1], (Y, Z)), 0.0),
                )
                delta += jnp.where(
                    last_z,
                    jnp.broadcast_to(high_z[:, at : at + 1], (Y, Z)),
                    jnp.where(first_z, -jnp.broadcast_to(low_z[:, at : at + 1], (Y, Z)), 0.0),
                )
                add(f, x, delta)
        if between is not None:
            between()
        wait_halo(k, 0)
        if k == 1:
            each_side(lambda copy: copy.wait_recv(), False)
            low, high = neighbour_flux(0), neighbour_flux(1)
        else:
            low, high = ([halo_x[k, side, f] for f in range(F)] for side in range(2))
        for f in range(F):
            add(f, 0, -low[f])
            add(f, X - 1, high[f])

    def owner_of(i, j, k):
        return owner_ref[patch_ref[j, k, i]]

    def row_of(o):
        ox = lax.div(o, n_gy * n_gz)
        return lax.rem(ox, 2) * n_gy + lax.rem(lax.div(o, n_gz), n_gy)

    def cell_of(o):
        return lax.rem(o, n_gz) * n_plane + lax.div(o, 2 * n_gy * n_gz)

    row_index = lax.broadcasted_iota(jnp.int32, (TILE, Z), 0)
    packed_row = lax.broadcasted_iota(jnp.int32, (ROWS, Z), 0)
    packed_half = lax.rem(lax.broadcasted_iota(jnp.int32, (ROWS, Z), 1), BZ) // (BZ // 2)

    def route_tables():
        owners = {}

        def owner(di, j, dk):
            if (di, j, dk) not in owners:
                i = jnp.clip(plane * 2 + di, 0, n_gx - 1)
                owners[di, j, dk] = owner_of(i, j, jnp.clip(gz + dk, 0, n_gz - 1))
            return owners[di, j, dk]

        lanes = lax.broadcasted_iota(jnp.int32, (1, n_row * ROWS), 1)
        targets = [jnp.full((1, n_row * ROWS), -1, jnp.int32) for _ in range(2)]
        for t in range(n_row):
            di, j = t // n_gy, t % n_gy
            bricks = [(0, di, j, 0, None)]
            bricks.append((1, di + 1, j, 0, plane < n_plane - 1 if di == 1 else None))
            bricks.append((2, di - 1, j, 0, plane > 0 if di == 0 else None))
            if j < n_gy - 1:
                bricks.append((3, di, j + 1, 0, None))
            if j > 0:
                bricks.append((4, di, j - 1, 0, None))
            bricks.append((5, di, j, 1, has_up[2]))
            bricks.append((6, di, j, -1, has_down[2]))
            for r, bi, bj, bk, there in bricks:
                cell = cell_of(owner(bi, bj, bk)) + r // ROWS * n_plane * n_gz
                if there is not None:
                    cell = jnp.where(there, cell, -1)
                at = t * ROWS + r % ROWS
                targets[r // ROWS] = jnp.where(lanes == at, cell, targets[r // ROWS])
        cells = lax.broadcasted_iota(jnp.int32, (2 * n_plane * n_gz, n_row * ROWS), 0)
        choose[...] = jnp.logical_or(cells == targets[0], cells == targets[1]).astype(jnp.float32)
        to_row = jnp.full((ROWS, Z), -1, jnp.int32)
        slots = packed_row + ROWS * packed_half
        places = [(me, None)]
        for d in range(3):
            places += [(ups[d], has_up[d]), (downs[d], has_down[d])]
        for r, (place, there) in enumerate(places):
            row = row_of(owner_of(*place))
            if there is not None:
                row = jnp.where(there, row, -1)
            to_row = jnp.where(slots == r, row, to_row)
        row_choice[...] = to_row
        spread_to = lax.broadcasted_iota(jnp.int32, (Z, Z), 1)
        spread[...] = (
            lax.broadcasted_iota(jnp.int32, (Z, Z), 0)
            == BZ * lax.rem(spread_to, BOXES) + lax.div(spread_to, BOXES)
        ).astype(jnp.float32)

    loads[5].wait()
    for side in range(2):
        x = (X - 1) * side
        for i, layer in enumerate((source[x], speed[0, x], pull[x], push[x], inverse[x])):
            layers[side, i] = layer

    for k in range(STAGES):
        for x in (0, X - 1):
            v = [fields[k, f, x] for f in range(F)]
            q = flux(v, joint_term(v, x), x, 0)
            for f in range(F):
                flux_x[k, x, f] = q[f]
        if k == 0:
            pl.semaphore_wait(barrier, expected)
        if k != 1:
            send_halo(k, 0)
        packs = [jnp.zeros((Y, Z), jnp.float32), jnp.zeros((Y, Z), jnp.float32)]
        for x in range(X):
            v = [fields[k, f, x] for f in range(F)]
            joint = joint_term(v, x)
            if 0 < x < X - 1:
                q = flux(v, joint, x, 0)
                for f in range(F):
                    flux_x[k, x, f] = q[f]
            q = flux(v, joint, x, 2)
            columns = q + [source[x]] if k == 0 else q
            for f, column in enumerate(columns):
                here = lane == f * X + x
                packs[0] = jnp.where(here, jnp.broadcast_to(column[:, 0:1], (Y, Z)), packs[0])
                packs[1] = jnp.where(here, jnp.broadcast_to(column[:, Z - 1 : Z], (Y, Z)), packs[1])
            for f in range(F):
                fields[k + 1, f, x] = (
                    damp[x] * v[f]
                    + jnp.where(last_z, 0.0, pltpu.roll(q[f], Z - 1, 1))
                    - jnp.where(first_z, 0.0, pltpu.roll(q[f], 1, 1))
                )
            q = flux(v, joint, x, 1)
            if k == 0:
                flux_y[k, F, pl.ds(x * Y, Y), :] = source[x]
            for f in range(F):
                flux_y[k, f, pl.ds(x * Y, Y), :] = q[f]
                fields[k + 1, f, x] += jnp.where(last_y, 0.0, pltpu.roll(q[f], Y - 1, 0)) - jnp.where(
                    first_y, 0.0, pltpu.roll(q[f], 1, 0)
                )
        for side in range(2):
            send_z[k, side] = packs[side]
        send_halo(k, 2)
        for f in range(F + 1 if k == 0 else F):
            for side in range(2):
                send_y[k, side, f] = flux_y[k, f, pl.ds((Y - 1) * side, X, stride=Y), :]
        send_halo(k, 1)
        for x in range(X):
            for f in range(F):
                if x == 0:
                    fields[k + 1, f, x] += flux_x[k, x + 1, f]
                elif x == X - 1:
                    fields[k + 1, f, x] -= flux_x[k, x - 1, f]
                else:
                    fields[k + 1, f, x] += flux_x[k, x + 1, f] - flux_x[k, x - 1, f]
        if k == 0:
            each_side(lambda copy: copy.start(), True)
            send_tokens(1)
            loads[7].wait()
            loads[8].wait()
            route_tables()
            wait_tokens(1)
            send_tokens(2)
        if k < STAGES - 1:

            def add(f, x, delta):
                fields[k + 1, f, x] += delta

            def pass_line():
                wait_line(0)
                send_line(1)

            if k == 1:
                wait_tokens(2)
                send_line(0)
            finish_halo(k, add, pass_line if k == 1 else None)

    sixth = 0.5 * third
    tiles = []
    for f in range(F):
        total = jnp.zeros((Y, Z), jnp.float32)
        for x in range(X):
            value = third * fields[0, f, x] + 0.5 * fields[1, f, x] + sixth * fields[STAGES, f, x]
            result[f, x] = value
            total += value * source[x]
        weighted = [
            total,
            -sixth * flux_x[STAGES - 1, X - 1, f] * halo_layers[1, 0],
            sixth * flux_x[STAGES - 1, 0, f] * halo_layers[0, 0],
            -sixth * send_y[STAGES - 1, 1, f] * halo_y[0, 1, F],
            sixth * send_y[STAGES - 1, 0, f] * halo_y[0, 0, F],
        ]
        tile = jnp.zeros((TILE, Z), jnp.float32)
        for r, product in enumerate(weighted):
            line = jnp.sum(product, axis=0, keepdims=True)
            tile = jnp.where(row_index == r, jnp.broadcast_to(line, (TILE, Z)), tile)
        tiles.append(tile)

    block = jnp.zeros((TILE, Z), jnp.float32)
    for f in range(F):
        tile = tiles[f]
        for shift in (1, 2, 4, 8):
            tile = tile + pltpu.roll(tile, Z - shift, 1)
        if f:
            tile = pltpu.roll(tile, f, 1)
        block = jnp.where(lax.rem(lane, BZ) == f, tile, block)
    for side, row, sign in ((1, 5, -sixth), (0, 6, sixth)):
        shape = halo_z[0, side]
        shapes = jnp.zeros((Y, Z), jnp.float32)
        for f in range(F):
            moved = pltpu.roll(shape, Z - (F - f) * X, 1)
            shapes = jnp.where(lax.div(lane, X) == f, moved, shapes)
        line = jnp.broadcast_to(
            jnp.sum(sign * send_z[STAGES - 1, side] * shapes, axis=0, keepdims=True), (TILE, Z)
        )
        for shift in (1, 2, 4):
            line = line + pltpu.roll(line, Z - shift, 1)
        box = 0 if side else Z - BZ
        for f in range(F):
            moved = pltpu.roll(line, (box + f - f * X) % Z, 1)
            block = jnp.where(jnp.logical_and(row_index == row, lane == box + f), moved, block)
    block = step_length * block

    block = jnp.where(packed_half == 0, block[:ROWS], pltpu.roll(block, BZ // 2, 1)[ROWS:])
    to_row = row_choice[...]
    for t in range(n_row):
        row_send[t] = jnp.where(to_row == t, block, 0.0)

    def ring_copy(n, mine, device, src, dst, sems, r):
        t = lax.rem(mine + r, n)
        return pltpu.make_async_remote_copy(
            src_ref=src.at[t],
            dst_ref=dst.at[mine],
            send_sem=sems[0].at[r],
            recv_sem=sems[1].at[r],
            device_id=device(t),
            device_id_type=MESH,
        )

    row_copy = functools.partial(
        ring_copy, n_row, my_row, row_device, row_send, row_recv, (row_send_sem, row_recv_sem)
    )

    def cell_copy(dz, dy):
        return pltpu.make_async_remote_copy(
            src_ref=cell_send.at[cell_row(dz, dy)],
            dst_ref=cell_recv.at[my_cell],
            send_sem=cell_send_sem.at[dz * n_gz + dy],
            recv_sem=cell_recv_sem.at[dz * n_gz + dy],
            device_id=cell_device(dz, dy),
            device_id_type=MESH,
        )

    def far_first(n):
        return sorted(range(1, n), key=lambda r: -min(r, n - r))

    for r in far_first(n_row):
        row_copy(r).start()
    row_recv[my_row] = row_send[my_row]
    wait_line(1)
    send_line(2)
    for r in range(1, n_row):
        row_copy(r).wait_recv()
    rows = jnp.concatenate([row_recv[t] for t in range(n_row)], axis=0)
    cells = jnp.dot(
        choose[...], rows, preferred_element_type=jnp.float32, precision=lax.Precision.HIGHEST
    )
    n_cell = n_gz * n_plane
    first_half = lax.rem(lax.broadcasted_iota(jnp.int32, (n_cell, Z), 1), BZ) < BZ // 2
    moved = jnp.where(first_half, 0.0, cells[n_cell:])
    cells = jnp.where(first_half, cells[:n_cell], 0.0) + pltpu.roll(moved, Z - BZ // 2, 1)
    for t in range(n_cell):
        cell_send[t] = cells[t : t + 1]
    wait_line(2)
    hops = [0] + far_first(n_gz)
    others = [(dz % n_plane, dy) for dz in range(1, n_plane + 1) for dy in hops]
    others.remove((0, 0))
    for dz, dy in others:
        cell_copy(dz, dy).start()
    cell_recv[my_cell] = cell_send[my_cell]

    def add_result(f, x, delta):
        result[f, x] += sixth * delta

    finish_halo(STAGES - 1, add_result)
    for k in range(STAGES):
        for d in range(3):
            for side, has in ((1, has_up[d]), (0, has_down[d])):

                @pl.when(has)
                def _(side=side, k=k, d=d):
                    halo_copy(k, d, side).wait_send()

    each_side(lambda copy: copy.wait_send(), True)

    for r in range(1, n_row):
        row_copy(r).wait_send()
    for dz, dy in others:
        cell_copy(dz, dy).wait_recv()
    own = jnp.sum(cell_recv[...].reshape(n_gz * n_plane, Z), axis=0, keepdims=True)
    ordered = jnp.dot(
        own, spread[...], preferred_element_type=jnp.float32, precision=lax.Precision.HIGHEST
    )
    grad_ref[...] = ordered[:, : F * BOXES]
    for dz, dy in others:
        cell_copy(dz, dy).wait_send()


def solution(mesh):
    sizes = tuple(mesh.shape[axis] for axis in AXES)
    n_row = 2 * sizes[1]
    n_plane = sizes[0] // 2
    n_gz = sizes[2]

    def body(
        terminal_adjoint,
        density,
        velocity,
        stiffness,
        sponge,
        source_shape,
        brick_level,
        brick_patch,
        patch_owner,
    ):
        f32 = jnp.float32
        hbm = pl.BlockSpec(memory_space=pl.ANY)
        return pl.pallas_call(
            functools.partial(kernel, sizes),
            out_shape=(
                pltpu.VMEM((F, X, Y, Z), f32),
                pltpu.VMEM((1, F * BOXES), f32),
            ),
            in_specs=[hbm] * 9,
            out_specs=(pl.BlockSpec(memory_space=pltpu.VMEM),) * 2,
            scratch_shapes=[
                pltpu.SMEM((sizes[1], sizes[2], sizes[0]), jnp.int32),
                pltpu.SMEM((sizes[1], sizes[2], sizes[0]), jnp.int32),
                pltpu.SMEM((sizes[0] * sizes[1] * sizes[2],), jnp.int32),
                pltpu.VMEM((STAGES + 1, F, X, Y, Z), f32),
                pltpu.VMEM((X, Y, Z), f32),
                pltpu.VMEM((3, X, Y, Z), f32),
                pltpu.VMEM((X, Y, Z), f32),
                pltpu.VMEM((X, Y, Z), f32),
                pltpu.VMEM((X, Y, Z), f32),
                pltpu.VMEM((3, X, Y, Z), f32),
                pltpu.VMEM((X, Y, Z), f32),
                pltpu.VMEM((X, Y, Z), f32),
                pltpu.VMEM((X, Y, Z), f32),
                pltpu.VMEM((X, Y, Z), f32),
                pltpu.VMEM((STAGES, X, F, Y, Z), f32),
                pltpu.VMEM((STAGES, F + 1, X * Y, Z), f32),
                pltpu.VMEM((STAGES, 2, F + 1, X, Z), f32),
                pltpu.VMEM((STAGES, 2, Y, Z), f32),
                pltpu.VMEM((STAGES, 2, F, Y, Z), f32),
                pltpu.VMEM((STAGES, 2, F + 1, X, Z), f32),
                pltpu.VMEM((STAGES, 2, Y, Z), f32),
                pltpu.VMEM((2, F, Y, Z), f32),
                pltpu.VMEM((2, LAYERS, Y, Z), f32),
                pltpu.VMEM((2, LAYERS, Y, Z), f32),
                pltpu.VMEM((2 * n_plane * n_gz, n_row * ROWS), f32),
                pltpu.VMEM((ROWS, Z), jnp.int32),
                pltpu.VMEM((Z, Z), f32),
                pltpu.VMEM((n_row, ROWS, Z), f32),
                pltpu.VMEM((n_row, ROWS, Z), f32),
                pltpu.VMEM((n_plane * n_gz, 1, Z), f32),
                pltpu.VMEM((n_plane * n_gz, 1, Z), f32),
                pltpu.SemaphoreType.DMA((9,)),
                pltpu.SemaphoreType.DMA((STAGES, 3, 2)),
                pltpu.SemaphoreType.DMA((STAGES, 3, 2)),
                pltpu.SemaphoreType.DMA((2,)),
                pltpu.SemaphoreType.DMA((2,)),
                pltpu.SemaphoreType.DMA((n_row,)),
                pltpu.SemaphoreType.DMA((n_row,)),
                pltpu.SemaphoreType.DMA((n_plane * n_gz,)),
                pltpu.SemaphoreType.DMA((n_plane * n_gz,)),
                pltpu.SemaphoreType.REGULAR((2, 2)),
                pltpu.SemaphoreType.REGULAR((3,)),
            ],
            compiler_params=pltpu.CompilerParams(collective_id=0, has_side_effects=True),
        )(
            jnp.transpose(brick_level, (1, 2, 0)),
            jnp.transpose(brick_patch, (1, 2, 0)),
            patch_owner,
            terminal_adjoint,
            density,
            velocity,
            stiffness,
            sponge,
            source_shape,
        )

    in_specs = (
        P(None, "gx", "gy", "gz"),
        P("gx", "gy", "gz"),
        P(None, "gx", "gy", "gz"),
        P("gx", "gy", "gz"),
        P("gx", "gy", "gz"),
        P("gx", "gy", "gz"),
        P(),
        P(),
        P(),
    )
    out_specs = (P(None, "gx", "gy", "gz"), P(AXES, None))
    return jax.shard_map(body, mesh=mesh, in_specs=in_specs, out_specs=out_specs, check_vma=False)
```

```python
import functools

import jax
import jax.numpy as jnp
from jax import lax
from jax.experimental import pallas as pl
from jax.experimental.pallas import tpu as pltpu
from jax.sharding import PartitionSpec as P

MESH = pl.DeviceIdType.MESH
F = 5
X = 8
Y = 8
Z = 128
BZ = 16
BOXES = Z // BZ
TILE = 8
ROWS = TILE // 2
PARTS = 3
LAYERS = 5
STAGES = 3
step_length = 0.14
third = 1.0 / 3.0
AXES = ("gx", "gy", "gz")


def kernel(
    sizes,
    level_hbm,
    patch_hbm,
    owner_hbm,
    adjoint_hbm,
    density_hbm,
    velocity_hbm,
    stiffness_hbm,
    sponge_hbm,
    source_hbm,
    result,
    grad_ref,
    level_ref,
    patch_ref,
    owner_ref,
    fields,
    density,
    velocity,
    stiffness,
    sponge,
    source,
    speed,
    pull,
    push,
    inverse,
    damp,
    flux_x,
    flux_y,
    send_y,
    send_z,
    halo_x,
    halo_y,
    halo_z,
    send_x,
    layers,
    halo_layers,
    choose,
    row_choice,
    row_send,
    row_recv,
    cell_send,
    cell_recv,
    load_sem,
    halo_send_sem,
    halo_recv_sem,
    layer_send_sem,
    layer_recv_sem,
    row_send_sem,
    row_recv_sem,
    cell_send_sem,
    cell_recv_sem,
    token_sem,
    line_sem,
):
    n_gx, n_gy, n_gz = sizes
    gx, gy, gz = (lax.axis_index(axis) for axis in AXES)
    half = lax.rem(gx, 2)
    plane = lax.div(gx, 2)
    n_plane = n_gx // 2
    n_row = 2 * n_gy
    my_row = half * n_gy + gy
    my_cell = gz * n_plane + plane

    def row_device(t):
        return (plane * 2 + lax.div(t, n_gy), lax.rem(t, n_gy), gz)

    def column_device(t):
        return (gx, gy, t)

    def plane_device(t):
        return (t * 2 + half, gy, gz)

    def cell_device(dz, dy):
        return (lax.rem(plane + dz, n_plane) * 2 + half, gy, lax.rem(gz + dy, n_gz))

    def cell_row(dz, dy):
        return lax.rem(gz + dy, n_gz) * n_plane + lax.rem(plane + dz, n_plane)

    barrier = pltpu.get_barrier_semaphore()
    me = (gx, gy, gz)
    ups, downs, has_up, has_down = [], [], [], []
    for d in range(3):
        up, down = list(me), list(me)
        up[d] = jnp.minimum(me[d] + 1, sizes[d] - 1)
        down[d] = jnp.maximum(me[d] - 1, 0)
        ups.append(tuple(up))
        downs.append(tuple(down))
        has_up.append(me[d] < sizes[d] - 1)
        has_down.append(me[d] > 0)

    loads = []
    for i, (src, dst) in enumerate(
        (
            (density_hbm, density),
            (velocity_hbm, velocity),
            (stiffness_hbm, stiffness),
            (sponge_hbm, sponge),
            (adjoint_hbm, fields.at[0]),
            (source_hbm, source),
            (level_hbm, level_ref),
            (patch_hbm, patch_ref),
            (owner_hbm, owner_ref),
        )
    ):
        copy = pltpu.make_async_copy(src, dst, load_sem.at[i])
        copy.start()
        loads.append(copy)

    def greet(to):
        pl.semaphore_signal(barrier, inc=1, device_id=to, device_id_type=MESH)

    cross_up = jnp.logical_and(half == 1, has_up[0])
    cross_down = jnp.logical_and(half == 0, has_down[0])
    for has, to in ((cross_up, ups[0]), (cross_down, downs[0])):

        @pl.when(has)
        def _(to=to):
            greet(to)

    rings = (
        (n_row, my_row, row_device, (n_row // 2, 1, n_row - 1)),
        (n_gz, gz, column_device, (1, n_gz - 1)),
    )
    for n, mine, device, near in rings:
        for r in near:
            greet(device(lax.rem(mine + r, n)))

    def planes_at(step):
        up, down = plane + step, plane - step
        return (
            (up < n_plane, plane_device(jnp.minimum(up, n_plane - 1))),
            (down >= 0, plane_device(jnp.maximum(down, 0))),
        )

    def line_count(step):
        return sum(jnp.where(has, 1, 0) for has, _ in planes_at(step))

    for has, to in planes_at(1):

        @pl.when(has)
        def _(to=to):
            greet(to)

    expected = (
        jnp.int32(sum(len(near) for _, _, _, near in rings))
        + line_count(1)
        + jnp.where(cross_up, 1, 0)
        + jnp.where(cross_down, 1, 0)
    )

    def send_tokens(level):
        for ring, (n, mine, device, _) in enumerate(rings):
            for r in (level, n - level):
                pl.semaphore_signal(
                    token_sem.at[ring, level - 1],
                    inc=1,
                    device_id=device(lax.rem(mine + r, n)),
                    device_id_type=MESH,
                )

    def wait_tokens(level):
        for ring in range(len(rings)):
            pl.semaphore_wait(token_sem.at[ring, level - 1], 2)

    def send_line(level):
        for has, to in planes_at(1 << level):

            @pl.when(has)
            def _(to=to):
                pl.semaphore_signal(
                    line_sem.at[level], inc=1, device_id=to, device_id_type=MESH
                )

    def wait_line(level):
        pl.semaphore_wait(line_sem.at[level], line_count(1 << level))

    for d, halo in enumerate((halo_x, halo_y, halo_z)):
        for side, has in ((0, has_down[d]), (1, has_up[d])):

            @pl.when(jnp.logical_not(has))
            def _(halo=halo, side=side):
                for k in range(STAGES):
                    halo[k, side] = jnp.zeros(halo.shape[2:], jnp.float32)
                if halo is halo_x:
                    halo_layers[side] = jnp.zeros(halo_layers.shape[1:], jnp.float32)

    loads[6].wait()
    level = level_ref[gy, gz, gx]
    scale = 0.5 * step_length * lax.shift_left(jnp.int32(1), level).astype(jnp.float32)
    for copy in loads[:4]:
        copy.wait()
    for x in range(X):
        rho = density[x]
        speed[:, x] = scale * velocity[:, x]
        pull[x] = scale * rho
        push[x] = scale * stiffness[x]
        inverse[x] = scale / rho
        damp[x] = 1.0 - step_length * sponge[x]
    loads[4].wait()

    sub = lax.broadcasted_iota(jnp.int32, (Y, Z), 0)
    lane = lax.broadcasted_iota(jnp.int32, (Y, Z), 1)
    first_y, last_y = sub == 0, sub == Y - 1
    first_z, last_z = lane == 0, lane == Z - 1

    def flux(v, joint, x, d):
        c = speed[d, x]
        q = [c * v[f] for f in range(F)]
        q[1 + d] = q[1 + d] + joint
        q[4] = q[4] + inverse[x] * v[1 + d]
        return q

    def joint_term(v, x):
        return pull[x] * v[0] + push[x] * v[4]

    def halo_copy(k, d, side):
        parts = pl.ds(0, F + 1 if k == 0 else F)
        if d == 0:
            src = send_x.at[side] if k == 1 else flux_x.at[k, (X - 1) * side]
            dst = halo_x.at[k, 1 - side]
        elif d == 1:
            src, dst = send_y.at[k, side, parts], halo_y.at[k, 1 - side, parts]
        else:
            src, dst = send_z.at[k, side], halo_z.at[k, 1 - side]
        return pltpu.make_async_remote_copy(
            src_ref=src,
            dst_ref=dst,
            send_sem=halo_send_sem.at[k, d, side],
            recv_sem=halo_recv_sem.at[k, d, 1 - side],
            device_id=ups[d] if side else downs[d],
            device_id_type=MESH,
        )

    def send_halo(k, d):
        for side, has in ((1, has_up[d]), (0, has_down[d])):

            @pl.when(has)
            def _(side=side):
                halo_copy(k, d, side).start()

    def wait_halo(k, d):
        for side, has in ((1, has_down[d]), (0, has_up[d])):

            @pl.when(has)
            def _(side=side):
                halo_copy(k, d, side).wait_recv()

    def layer_copy(side):
        return pltpu.make_async_remote_copy(
            src_ref=layers.at[side],
            dst_ref=halo_layers.at[1 - side],
            send_sem=layer_send_sem.at[side],
            recv_sem=layer_recv_sem.at[1 - side],
            device_id=ups[0] if side else downs[0],
            device_id_type=MESH,
        )

    def each_side(act, up_first):
        for side in (1, 0):
            has = (has_up if (side == 1) == up_first else has_down)[0]

            @pl.when(has)
            def _(side=side):
                act(layer_copy(side))

    def send_outermost():
        for side in range(2):
            for f in range(F):
                send_x[side, f] = fields[1, f, (X - 1) * side]
        send_halo(1, 0)

    def neighbour_flux(side):
        at, sign = ((0, 1.0), (X - 1, -1.0))[side]
        v = [halo_x[1, side, f] + sign * flux_x[0, at, f] for f in range(F)]
        q = [halo_layers[side, 1] * v[f] for f in range(F)]
        q[1] = q[1] + (halo_layers[side, 2] * v[0] + halo_layers[side, 3] * v[4])
        q[4] = q[4] + halo_layers[side, 4] * v[1]
        return q

    def finish_halo(k, add, between=None):
        wait_halo(k, 1)
        wait_halo(k, 2)
        low_z, high_z = halo_z[k, 0], halo_z[k, 1]
        for x in (0, X - 1, *range(1, X - 1)):
            if k == 0 and x == 1:
                send_outermost()
            for f in range(F):
                low_y, high_y = halo_y[k, 0, f], halo_y[k, 1, f]
                at = f * X + x
                delta = jnp.where(
                    last_y,
                    jnp.broadcast_to(high_y[x : x + 1], (Y, Z)),
                    jnp.where(first_y, -jnp.broadcast_to(low_y[x : x + 1], (Y, Z)), 0.0),
                )
                delta += jnp.where(
                    last_z,
                    jnp.broadcast_to(high_z[:, at : at + 1], (Y, Z)),
                    jnp.where(first_z, -jnp.broadcast_to(low_z[:, at : at + 1], (Y, Z)), 0.0),
                )
                add(f, x, delta)
        if between is not None:
            between()
        wait_halo(k, 0)
        if k == 1:
            each_side(lambda copy: copy.wait_recv(), False)
            low, high = neighbour_flux(0), neighbour_flux(1)
        else:
            low, high = ([halo_x[k, side, f] for f in range(F)] for side in range(2))
        for f in range(F):
            add(f, 0, -low[f])
            add(f, X - 1, high[f])

    def owner_of(i, j, k):
        return owner_ref[patch_ref[j, k, i]]

    def row_of(o):
        ox = lax.div(o, n_gy * n_gz)
        return lax.rem(ox, 2) * n_gy + lax.rem(lax.div(o, n_gz), n_gy)

    def cell_of(o):
        return lax.rem(o, n_gz) * n_plane + lax.div(o, 2 * n_gy * n_gz)

    row_index = lax.broadcasted_iota(jnp.int32, (TILE, Z), 0)
    packed_row = lax.broadcasted_iota(jnp.int32, (ROWS, Z), 0)
    packed_half = lax.rem(lax.broadcasted_iota(jnp.int32, (ROWS, Z), 1), BZ) // (BZ // 2)

    def route_tables():
        owners = {}

        def owner(di, j, dk):
            if (di, j, dk) not in owners:
                i = jnp.clip(plane * 2 + di, 0, n_gx - 1)
                owners[di, j, dk] = owner_of(i, j, jnp.clip(gz + dk, 0, n_gz - 1))
            return owners[di, j, dk]

        shape = (1, PARTS * n_row * ROWS)
        lanes = lax.rem(lax.broadcasted_iota(jnp.int32, shape, 1), n_row * ROWS)
        targets = [jnp.full(shape, -1, jnp.int32) for _ in range(2)]
        for t in range(n_row):
            di, j = t // n_gy, t % n_gy
            bricks = [(0, di, j, 0, None)]
            bricks.append((1, di + 1, j, 0, plane < n_plane - 1 if di == 1 else None))
            bricks.append((2, di - 1, j, 0, plane > 0 if di == 0 else None))
            if j < n_gy - 1:
                bricks.append((3, di, j + 1, 0, None))
            if j > 0:
                bricks.append((4, di, j - 1, 0, None))
            bricks.append((5, di, j, 1, has_up[2]))
            bricks.append((6, di, j, -1, has_down[2]))
            for r, bi, bj, bk, there in bricks:
                cell = cell_of(owner(bi, bj, bk)) + r // ROWS * n_plane * n_gz
                if there is not None:
                    cell = jnp.where(there, cell, -1)
                at = t * ROWS + r % ROWS
                targets[r // ROWS] = jnp.where(lanes == at, cell, targets[r // ROWS])
        cells = lax.broadcasted_iota(jnp.int32, choose.shape, 0)
        chosen = jnp.logical_or(cells == targets[0], cells == targets[1])
        choose[...] = jnp.where(chosen, 1.0, 0.0).astype(jnp.bfloat16)
        to_row = jnp.full((ROWS, Z), -1, jnp.int32)
        slots = packed_row + ROWS * packed_half
        places = [(me, None)]
        for d in range(3):
            places += [(ups[d], has_up[d]), (downs[d], has_down[d])]
        for r, (place, there) in enumerate(places):
            row = row_of(owner_of(*place))
            if there is not None:
                row = jnp.where(there, row, -1)
            to_row = jnp.where(slots == r, row, to_row)
        row_choice[...] = to_row

    loads[5].wait()
    for side in range(2):
        x = (X - 1) * side
        for i, layer in enumerate((source[x], speed[0, x], pull[x], push[x], inverse[x])):
            layers[side, i] = layer

    for k in range(STAGES):
        for x in (0, X - 1):
            v = [fields[k, f, x] for f in range(F)]
            q = flux(v, joint_term(v, x), x, 0)
            for f in range(F):
                flux_x[k, x, f] = q[f]
        if k == 0:
            pl.semaphore_wait(barrier, expected)
        if k != 1:
            send_halo(k, 0)
        packs = [jnp.zeros((Y, Z), jnp.float32), jnp.zeros((Y, Z), jnp.float32)]
        for x in range(X):
            v = [fields[k, f, x] for f in range(F)]
            joint = joint_term(v, x)
            if 0 < x < X - 1:
                q = flux(v, joint, x, 0)
                for f in range(F):
                    flux_x[k, x, f] = q[f]
            q = flux(v, joint, x, 2)
            columns = q + [source[x]] if k == 0 else q
            for f, column in enumerate(columns):
                here = lane == f * X + x
                packs[0] = jnp.where(here, jnp.broadcast_to(column[:, 0:1], (Y, Z)), packs[0])
                packs[1] = jnp.where(here, jnp.broadcast_to(column[:, Z - 1 : Z], (Y, Z)), packs[1])
            for f in range(F):
                fields[k + 1, f, x] = (
                    damp[x] * v[f]
                    + jnp.where(last_z, 0.0, pltpu.roll(q[f], Z - 1, 1))
                    - jnp.where(first_z, 0.0, pltpu.roll(q[f], 1, 1))
                )
            q = flux(v, joint, x, 1)
            if k == 0:
                flux_y[k, F, pl.ds(x * Y, Y), :] = source[x]
            for f in range(F):
                flux_y[k, f, pl.ds(x * Y, Y), :] = q[f]
                fields[k + 1, f, x] += jnp.where(last_y, 0.0, pltpu.roll(q[f], Y - 1, 0)) - jnp.where(
                    first_y, 0.0, pltpu.roll(q[f], 1, 0)
                )
        for side in range(2):
            send_z[k, side] = packs[side]
        send_halo(k, 2)
        for f in range(F + 1 if k == 0 else F):
            for side in range(2):
                send_y[k, side, f] = flux_y[k, f, pl.ds((Y - 1) * side, X, stride=Y), :]
        send_halo(k, 1)
        for x in range(X):
            for f in range(F):
                if x == 0:
                    fields[k + 1, f, x] += flux_x[k, x + 1, f]
                elif x == X - 1:
                    fields[k + 1, f, x] -= flux_x[k, x - 1, f]
                else:
                    fields[k + 1, f, x] += flux_x[k, x + 1, f] - flux_x[k, x - 1, f]
        if k == 0:
            each_side(lambda copy: copy.start(), True)
            send_tokens(1)
            loads[7].wait()
            loads[8].wait()
            route_tables()
            wait_tokens(1)
            send_tokens(2)
        if k < STAGES - 1:

            def add(f, x, delta):
                fields[k + 1, f, x] += delta

            def pass_line():
                wait_line(0)
                send_line(1)

            if k == 1:
                wait_tokens(2)
                send_line(0)
            finish_halo(k, add, pass_line if k == 1 else None)

    sixth = 0.5 * third
    tiles = []
    for f in range(F):
        total = jnp.zeros((Y, Z), jnp.float32)
        for x in range(X):
            value = third * fields[0, f, x] + 0.5 * fields[1, f, x] + sixth * fields[STAGES, f, x]
            result[f, x] = value
            total += value * source[x]
        weighted = [
            total,
            -sixth * flux_x[STAGES - 1, X - 1, f] * halo_layers[1, 0],
            sixth * flux_x[STAGES - 1, 0, f] * halo_layers[0, 0],
            -sixth * send_y[STAGES - 1, 1, f] * halo_y[0, 1, F],
            sixth * send_y[STAGES - 1, 0, f] * halo_y[0, 0, F],
        ]
        tile = jnp.zeros((TILE, Z), jnp.float32)
        for r, product in enumerate(weighted):
            line = jnp.sum(product, axis=0, keepdims=True)
            tile = jnp.where(row_index == r, jnp.broadcast_to(line, (TILE, Z)), tile)
        tiles.append(tile)

    block = jnp.zeros((TILE, Z), jnp.float32)
    for f in range(F):
        tile = tiles[f]
        for shift in (1, 2, 4, 8):
            tile = tile + pltpu.roll(tile, Z - shift, 1)
        if f:
            tile = pltpu.roll(tile, f, 1)
        block = jnp.where(lax.rem(lane, BZ) == f, tile, block)
    for side, row, sign in ((1, 5, -sixth), (0, 6, sixth)):
        shape = halo_z[0, side]
        shapes = jnp.zeros((Y, Z), jnp.float32)
        for f in range(F):
            moved = pltpu.roll(shape, Z - (F - f) * X, 1)
            shapes = jnp.where(lax.div(lane, X) == f, moved, shapes)
        line = jnp.broadcast_to(
            jnp.sum(sign * send_z[STAGES - 1, side] * shapes, axis=0, keepdims=True), (TILE, Z)
        )
        for shift in (1, 2, 4):
            line = line + pltpu.roll(line, Z - shift, 1)
        box = 0 if side else Z - BZ
        for f in range(F):
            moved = pltpu.roll(line, (box + f - f * X) % Z, 1)
            block = jnp.where(jnp.logical_and(row_index == row, lane == box + f), moved, block)
    block = step_length * block

    block = jnp.where(packed_half == 0, block[:ROWS], pltpu.roll(block, BZ // 2, 1)[ROWS:])
    to_row = row_choice[...]
    for t in range(n_row):
        row_send[t] = jnp.where(to_row == t, block, 0.0)

    def ring_copy(n, mine, device, src, dst, sems, r):
        t = lax.rem(mine + r, n)
        return pltpu.make_async_remote_copy(
            src_ref=src.at[t],
            dst_ref=dst.at[mine],
            send_sem=sems[0].at[r],
            recv_sem=sems[1].at[r],
            device_id=device(t),
            device_id_type=MESH,
        )

    row_copy = functools.partial(
        ring_copy, n_row, my_row, row_device, row_send, row_recv, (row_send_sem, row_recv_sem)
    )

    def cell_copy(dz, dy):
        return pltpu.make_async_remote_copy(
            src_ref=cell_send.at[cell_row(dz, dy)],
            dst_ref=cell_recv.at[my_cell],
            send_sem=cell_send_sem.at[dz * n_gz + dy],
            recv_sem=cell_recv_sem.at[dz * n_gz + dy],
            device_id=cell_device(dz, dy),
            device_id_type=MESH,
        )

    def far_first(n):
        return sorted(range(1, n), key=lambda r: -min(r, n - r))

    for r in far_first(n_row):
        row_copy(r).start()
    row_recv[my_row] = row_send[my_row]
    wait_line(1)
    send_line(2)
    for r in range(1, n_row):
        row_copy(r).wait_recv()
    rows = jnp.concatenate([row_recv[t] for t in range(n_row)], axis=0)
    parts = []
    for _ in range(PARTS):
        parts.append(rows.astype(jnp.bfloat16))
        rows = rows - parts[-1].astype(jnp.float32)
    cells = jnp.dot(
        choose[...], jnp.concatenate(parts, axis=0), preferred_element_type=jnp.float32
    )
    n_cell = n_gz * n_plane
    first_half = lax.rem(lax.broadcasted_iota(jnp.int32, (n_cell, Z), 1), BZ) < BZ // 2
    moved = jnp.where(first_half, 0.0, cells[n_cell:])
    cells = jnp.where(first_half, cells[:n_cell], 0.0) + pltpu.roll(moved, Z - BZ // 2, 1)
    for t in range(n_cell):
        cell_send[t] = cells[t : t + 1]
    wait_line(2)
    hops = [0] + far_first(n_gz)
    others = [(dz % n_plane, dy) for dz in range(1, n_plane + 1) for dy in hops]
    others.remove((0, 0))
    for dz, dy in others:
        cell_copy(dz, dy).start()
    cell_recv[my_cell] = cell_send[my_cell]

    def add_result(f, x, delta):
        result[f, x] += sixth * delta

    finish_halo(STAGES - 1, add_result)
    for k in range(STAGES):
        for d in range(3):
            for side, has in ((1, has_up[d]), (0, has_down[d])):

                @pl.when(has)
                def _(side=side, k=k, d=d):
                    halo_copy(k, d, side).wait_send()

    each_side(lambda copy: copy.wait_send(), True)

    for r in range(1, n_row):
        row_copy(r).wait_send()
    for dz, dy in others:
        cell_copy(dz, dy).wait_recv()
    own = jnp.sum(cell_recv[...].reshape(n_gz * n_plane, Z), axis=0, keepdims=True)
    grad_ref[...] = own
    for dz, dy in others:
        cell_copy(dz, dy).wait_send()


def write_out(fields, row, fields_out, gradient_out, gradient, sems):
    copy = pltpu.make_async_copy(fields, fields_out, sems.at[0])
    copy.start()
    to = lax.broadcasted_iota(jnp.int32, (TILE, Z), 1)
    place = BZ * lax.rem(to, BOXES) + lax.div(to, BOXES)
    wide = jnp.broadcast_to(row[...], (TILE, Z))
    gradient[...] = jnp.take_along_axis(wide, place, axis=1)[:1, : F * BOXES]
    small = pltpu.make_async_copy(gradient, gradient_out, sems.at[1])
    small.start()
    copy.wait()
    small.wait()


def solution(mesh):
    sizes = tuple(mesh.shape[axis] for axis in AXES)
    n_row = 2 * sizes[1]
    n_plane = sizes[0] // 2
    n_gz = sizes[2]

    def body(
        terminal_adjoint,
        density,
        velocity,
        stiffness,
        sponge,
        source_shape,
        brick_level,
        brick_patch,
        patch_owner,
    ):
        f32 = jnp.float32
        hbm = pl.BlockSpec(memory_space=pl.ANY)
        fields, gradient = pl.pallas_call(
            functools.partial(kernel, sizes),
            out_shape=(
                pltpu.VMEM((F, X, Y, Z), f32),
                pltpu.VMEM((1, Z), f32),
            ),
            in_specs=[hbm] * 9,
            out_specs=(pl.BlockSpec(memory_space=pltpu.VMEM),) * 2,
            scratch_shapes=[
                pltpu.SMEM((sizes[1], sizes[2], sizes[0]), jnp.int32),
                pltpu.SMEM((sizes[1], sizes[2], sizes[0]), jnp.int32),
                pltpu.SMEM((sizes[0] * sizes[1] * sizes[2],), jnp.int32),
                pltpu.VMEM((STAGES + 1, F, X, Y, Z), f32),
                pltpu.VMEM((X, Y, Z), f32),
                pltpu.VMEM((3, X, Y, Z), f32),
                pltpu.VMEM((X, Y, Z), f32),
                pltpu.VMEM((X, Y, Z), f32),
                pltpu.VMEM((X, Y, Z), f32),
                pltpu.VMEM((3, X, Y, Z), f32),
                pltpu.VMEM((X, Y, Z), f32),
                pltpu.VMEM((X, Y, Z), f32),
                pltpu.VMEM((X, Y, Z), f32),
                pltpu.VMEM((X, Y, Z), f32),
                pltpu.VMEM((STAGES, X, F, Y, Z), f32),
                pltpu.VMEM((STAGES, F + 1, X * Y, Z), f32),
                pltpu.VMEM((STAGES, 2, F + 1, X, Z), f32),
                pltpu.VMEM((STAGES, 2, Y, Z), f32),
                pltpu.VMEM((STAGES, 2, F, Y, Z), f32),
                pltpu.VMEM((STAGES, 2, F + 1, X, Z), f32),
                pltpu.VMEM((STAGES, 2, Y, Z), f32),
                pltpu.VMEM((2, F, Y, Z), f32),
                pltpu.VMEM((2, LAYERS, Y, Z), f32),
                pltpu.VMEM((2, LAYERS, Y, Z), f32),
                pltpu.VMEM((2 * n_plane * n_gz, PARTS * n_row * ROWS), jnp.bfloat16),
                pltpu.VMEM((ROWS, Z), jnp.int32),
                pltpu.VMEM((n_row, ROWS, Z), f32),
                pltpu.VMEM((n_row, ROWS, Z), f32),
                pltpu.VMEM((n_plane * n_gz, 1, Z), f32),
                pltpu.VMEM((n_plane * n_gz, 1, Z), f32),
                pltpu.SemaphoreType.DMA((9,)),
                pltpu.SemaphoreType.DMA((STAGES, 3, 2)),
                pltpu.SemaphoreType.DMA((STAGES, 3, 2)),
                pltpu.SemaphoreType.DMA((2,)),
                pltpu.SemaphoreType.DMA((2,)),
                pltpu.SemaphoreType.DMA((n_row,)),
                pltpu.SemaphoreType.DMA((n_row,)),
                pltpu.SemaphoreType.DMA((n_plane * n_gz,)),
                pltpu.SemaphoreType.DMA((n_plane * n_gz,)),
                pltpu.SemaphoreType.REGULAR((2, 2)),
                pltpu.SemaphoreType.REGULAR((3,)),
            ],
            compiler_params=pltpu.CompilerParams(collective_id=0, has_side_effects=True),
        )(
            jnp.transpose(brick_level, (1, 2, 0)),
            jnp.transpose(brick_patch, (1, 2, 0)),
            patch_owner,
            terminal_adjoint,
            density,
            velocity,
            stiffness,
            sponge,
            source_shape,
        )
        return pl.pallas_call(
            write_out,
            out_shape=(
                jax.ShapeDtypeStruct((F, X, Y, Z), f32),
                jax.ShapeDtypeStruct((1, F * BOXES), f32),
            ),
            in_specs=[pl.BlockSpec(memory_space=pltpu.VMEM)] * 2,
            out_specs=(hbm, hbm),
            scratch_shapes=[pltpu.VMEM((1, F * BOXES), f32), pltpu.SemaphoreType.DMA((2,))],
        )(
            pltpu.with_memory_space_constraint(fields, pltpu.VMEM),
            pltpu.with_memory_space_constraint(gradient, pltpu.VMEM),
        )

    in_specs = (
        P(None, "gx", "gy", "gz"),
        P("gx", "gy", "gz"),
        P(None, "gx", "gy", "gz"),
        P("gx", "gy", "gz"),
        P("gx", "gy", "gz"),
        P("gx", "gy", "gz"),
        P(),
        P(),
        P(),
    )
    out_specs = (P(None, "gx", "gy", "gz"), P(AXES, None))
    return jax.shard_map(body, mesh=mesh, in_specs=in_specs, out_specs=out_specs, check_vma=False)
```

```python
import functools

import jax
import jax.numpy as jnp
from jax import lax
from jax.experimental import pallas as pl
from jax.experimental.pallas import tpu as pltpu
from jax.sharding import PartitionSpec as P

MESH = pl.DeviceIdType.MESH
F = 5
X = 8
Y = 8
Z = 128
BZ = 16
BOXES = Z // BZ
TILE = 8
ROWS = TILE // 2
PARTS = 3
LAYERS = 5
STAGES = 3
step_length = 0.14
third = 1.0 / 3.0
AXES = ("gx", "gy", "gz")


def kernel(
    sizes,
    level_hbm,
    patch_hbm,
    owner_hbm,
    adjoint_hbm,
    density_hbm,
    velocity_hbm,
    stiffness_hbm,
    sponge_hbm,
    source_hbm,
    result,
    grad_ref,
    level_ref,
    patch_ref,
    owner_ref,
    fields,
    density,
    velocity,
    stiffness,
    sponge,
    source,
    speed,
    pull,
    push,
    inverse,
    damp,
    flux_x,
    flux_y,
    send_y,
    send_z,
    halo_x,
    halo_y,
    halo_z,
    send_x,
    layers,
    halo_layers,
    choose,
    row_choice,
    row_send,
    row_recv,
    cell_send,
    cell_recv,
    load_sem,
    halo_send_sem,
    halo_recv_sem,
    layer_send_sem,
    layer_recv_sem,
    row_send_sem,
    row_recv_sem,
    cell_send_sem,
    cell_recv_sem,
    token_sem,
    line_sem,
):
    n_gx, n_gy, n_gz = sizes
    gx, gy, gz = (lax.axis_index(axis) for axis in AXES)
    half = lax.rem(gx, 2)
    plane = lax.div(gx, 2)
    n_plane = n_gx // 2
    n_row = 2 * n_gy
    my_row = half * n_gy + gy
    my_cell = gz * n_plane + plane

    def row_device(t):
        return (plane * 2 + lax.div(t, n_gy), lax.rem(t, n_gy), gz)

    def column_device(t):
        return (gx, gy, t)

    def plane_device(t):
        return (t * 2 + half, gy, gz)

    def cell_device(dz, dy):
        return (lax.rem(plane + dz, n_plane) * 2 + half, gy, lax.rem(gz + dy, n_gz))

    def cell_row(dz, dy):
        return lax.rem(gz + dy, n_gz) * n_plane + lax.rem(plane + dz, n_plane)

    barrier = pltpu.get_barrier_semaphore()
    me = (gx, gy, gz)
    ups, downs, has_up, has_down = [], [], [], []
    for d in range(3):
        up, down = list(me), list(me)
        up[d] = jnp.minimum(me[d] + 1, sizes[d] - 1)
        down[d] = jnp.maximum(me[d] - 1, 0)
        ups.append(tuple(up))
        downs.append(tuple(down))
        has_up.append(me[d] < sizes[d] - 1)
        has_down.append(me[d] > 0)

    loads = []
    for i, (src, dst) in enumerate(
        (
            (density_hbm, density),
            (velocity_hbm, velocity),
            (stiffness_hbm, stiffness),
            (sponge_hbm, sponge),
            (adjoint_hbm, fields.at[0]),
            (source_hbm, source),
            (level_hbm, level_ref),
            (patch_hbm, patch_ref),
            (owner_hbm, owner_ref),
        )
    ):
        copy = pltpu.make_async_copy(src, dst, load_sem.at[i])
        copy.start()
        loads.append(copy)

    def greet(to):
        pl.semaphore_signal(barrier, inc=1, device_id=to, device_id_type=MESH)

    cross_up = jnp.logical_and(half == 1, has_up[0])
    cross_down = jnp.logical_and(half == 0, has_down[0])
    for has, to in ((cross_up, ups[0]), (cross_down, downs[0])):

        @pl.when(has)
        def _(to=to):
            greet(to)

    rings = (
        (n_row, my_row, row_device, (n_row // 2, 1, n_row - 1)),
        (n_gz, gz, column_device, (1, n_gz - 1)),
    )
    for n, mine, device, near in rings:
        for r in near:
            greet(device(lax.rem(mine + r, n)))

    def planes_at(step):
        up, down = plane + step, plane - step
        return (
            (up < n_plane, plane_device(jnp.minimum(up, n_plane - 1))),
            (down >= 0, plane_device(jnp.maximum(down, 0))),
        )

    def line_count(step):
        return sum(jnp.where(has, 1, 0) for has, _ in planes_at(step))

    for has, to in planes_at(1):

        @pl.when(has)
        def _(to=to):
            greet(to)

    expected = (
        jnp.int32(sum(len(near) for _, _, _, near in rings))
        + line_count(1)
        + jnp.where(cross_up, 1, 0)
        + jnp.where(cross_down, 1, 0)
    )

    def send_tokens(level):
        for ring, (n, mine, device, _) in enumerate(rings):
            for r in (level, n - level):
                pl.semaphore_signal(
                    token_sem.at[ring, level - 1],
                    inc=1,
                    device_id=device(lax.rem(mine + r, n)),
                    device_id_type=MESH,
                )

    def wait_tokens(level):
        for ring in range(len(rings)):
            pl.semaphore_wait(token_sem.at[ring, level - 1], 2)

    def send_line(level):
        for has, to in planes_at(1 << level):

            @pl.when(has)
            def _(to=to):
                pl.semaphore_signal(
                    line_sem.at[level], inc=1, device_id=to, device_id_type=MESH
                )

    def wait_line(level):
        pl.semaphore_wait(line_sem.at[level], line_count(1 << level))

    for d, halo in enumerate((halo_x, halo_y, halo_z)):
        for side, has in ((0, has_down[d]), (1, has_up[d])):

            @pl.when(jnp.logical_not(has))
            def _(halo=halo, side=side):
                for k in range(STAGES):
                    halo[k, side] = jnp.zeros(halo.shape[2:], jnp.float32)
                if halo is halo_x:
                    halo_layers[side] = jnp.zeros(halo_layers.shape[1:], jnp.float32)

    loads[6].wait()
    level = level_ref[gy, gz, gx]
    scale = 0.5 * step_length * lax.shift_left(jnp.int32(1), level).astype(jnp.float32)
    for copy in loads[:4]:
        copy.wait()
    for x in range(X):
        rho = density[x]
        speed[:, x] = scale * velocity[:, x]
        pull[x] = scale * rho
        push[x] = scale * stiffness[x]
        inverse[x] = scale / rho
        damp[x] = 1.0 - step_length * sponge[x]
    loads[4].wait()

    sub = lax.broadcasted_iota(jnp.int32, (Y, Z), 0)
    lane = lax.broadcasted_iota(jnp.int32, (Y, Z), 1)
    first_y, last_y = sub == 0, sub == Y - 1
    first_z, last_z = lane == 0, lane == Z - 1

    def flux(v, joint, x, d):
        c = speed[d, x]
        q = [c * v[f] for f in range(F)]
        q[1 + d] = q[1 + d] + joint
        q[4] = q[4] + inverse[x] * v[1 + d]
        return q

    def joint_term(v, x):
        return pull[x] * v[0] + push[x] * v[4]

    def halo_copy(k, d, side):
        parts = pl.ds(0, F + 1 if k == 0 else F)
        if d == 0:
            src = send_x.at[side] if k == 1 else flux_x.at[k, (X - 1) * side]
            dst = halo_x.at[k, 1 - side]
        elif d == 1:
            src, dst = send_y.at[k, side, parts], halo_y.at[k, 1 - side, parts]
        else:
            src, dst = send_z.at[k, side], halo_z.at[k, 1 - side]
        return pltpu.make_async_remote_copy(
            src_ref=src,
            dst_ref=dst,
            send_sem=halo_send_sem.at[k, d, side],
            recv_sem=halo_recv_sem.at[k, d, 1 - side],
            device_id=ups[d] if side else downs[d],
            device_id_type=MESH,
        )

    def send_halo(k, d):
        for side, has in ((1, has_up[d]), (0, has_down[d])):

            @pl.when(has)
            def _(side=side):
                halo_copy(k, d, side).start()

    def wait_halo(k, d):
        for side, has in ((1, has_down[d]), (0, has_up[d])):

            @pl.when(has)
            def _(side=side):
                halo_copy(k, d, side).wait_recv()

    def layer_copy(side):
        return pltpu.make_async_remote_copy(
            src_ref=layers.at[side],
            dst_ref=halo_layers.at[1 - side],
            send_sem=layer_send_sem.at[side],
            recv_sem=layer_recv_sem.at[1 - side],
            device_id=ups[0] if side else downs[0],
            device_id_type=MESH,
        )

    def each_side(act, up_first):
        for side in (1, 0):
            has = (has_up if (side == 1) == up_first else has_down)[0]

            @pl.when(has)
            def _(side=side):
                act(layer_copy(side))

    def send_outermost():
        for side in range(2):
            for f in range(F):
                send_x[side, f] = fields[1, f, (X - 1) * side]
        send_halo(1, 0)

    def neighbour_flux(side):
        at, sign = ((0, 1.0), (X - 1, -1.0))[side]
        v = [halo_x[1, side, f] + sign * flux_x[0, at, f] for f in range(F)]
        q = [halo_layers[side, 1] * v[f] for f in range(F)]
        q[1] = q[1] + (halo_layers[side, 2] * v[0] + halo_layers[side, 3] * v[4])
        q[4] = q[4] + halo_layers[side, 4] * v[1]
        return q

    def finish_halo(k, add, between=None):
        wait_halo(k, 1)
        wait_halo(k, 2)
        low_z, high_z = halo_z[k, 0], halo_z[k, 1]
        for x in (0, X - 1, *range(1, X - 1)):
            if k == 0 and x == 1:
                send_outermost()
            for f in range(F):
                low_y, high_y = halo_y[k, 0, f], halo_y[k, 1, f]
                at = f * X + x
                delta = jnp.where(
                    last_y,
                    jnp.broadcast_to(high_y[x : x + 1], (Y, Z)),
                    jnp.where(first_y, -jnp.broadcast_to(low_y[x : x + 1], (Y, Z)), 0.0),
                )
                delta += jnp.where(
                    last_z,
                    jnp.broadcast_to(high_z[:, at : at + 1], (Y, Z)),
                    jnp.where(first_z, -jnp.broadcast_to(low_z[:, at : at + 1], (Y, Z)), 0.0),
                )
                add(f, x, delta)
        if between is not None:
            between()
        wait_halo(k, 0)
        if k == 1:
            each_side(lambda copy: copy.wait_recv(), False)
            low, high = neighbour_flux(0), neighbour_flux(1)
        else:
            low, high = ([halo_x[k, side, f] for f in range(F)] for side in range(2))
        for f in range(F):
            add(f, 0, -low[f])
            add(f, X - 1, high[f])

    def owner_of(i, j, k):
        return owner_ref[patch_ref[j, k, i]]

    def row_of(o):
        ox = lax.div(o, n_gy * n_gz)
        return lax.rem(ox, 2) * n_gy + lax.rem(lax.div(o, n_gz), n_gy)

    def cell_of(o):
        return lax.rem(o, n_gz) * n_plane + lax.div(o, 2 * n_gy * n_gz)

    row_index = lax.broadcasted_iota(jnp.int32, (TILE, Z), 0)
    packed_row = lax.broadcasted_iota(jnp.int32, (ROWS, Z), 0)
    packed_half = lax.rem(lax.broadcasted_iota(jnp.int32, (ROWS, Z), 1), BZ) // (BZ // 2)

    def route_tables():
        owners = {}

        def owner(di, j, dk):
            if (di, j, dk) not in owners:
                i = jnp.clip(plane * 2 + di, 0, n_gx - 1)
                owners[di, j, dk] = owner_of(i, j, jnp.clip(gz + dk, 0, n_gz - 1))
            return owners[di, j, dk]

        shape = (1, PARTS * n_row * ROWS)
        lanes = lax.rem(lax.broadcasted_iota(jnp.int32, shape, 1), n_row * ROWS)
        targets = [jnp.full(shape, -1, jnp.int32) for _ in range(2)]
        for t in range(n_row):
            di, j = t // n_gy, t % n_gy
            bricks = [(0, di, j, 0, None)]
            bricks.append((1, di + 1, j, 0, plane < n_plane - 1 if di == 1 else None))
            bricks.append((2, di - 1, j, 0, plane > 0 if di == 0 else None))
            if j < n_gy - 1:
                bricks.append((3, di, j + 1, 0, None))
            if j > 0:
                bricks.append((4, di, j - 1, 0, None))
            bricks.append((5, di, j, 1, has_up[2]))
            bricks.append((6, di, j, -1, has_down[2]))
            for r, bi, bj, bk, there in bricks:
                cell = cell_of(owner(bi, bj, bk)) + r // ROWS * n_plane * n_gz
                if there is not None:
                    cell = jnp.where(there, cell, -1)
                at = t * ROWS + r % ROWS
                targets[r // ROWS] = jnp.where(lanes == at, cell, targets[r // ROWS])
        cells = lax.broadcasted_iota(jnp.int32, choose.shape, 0)
        chosen = jnp.logical_or(cells == targets[0], cells == targets[1])
        choose[...] = jnp.where(chosen, 1.0, 0.0).astype(jnp.bfloat16)
        to_row = jnp.full((ROWS, Z), -1, jnp.int32)
        slots = packed_row + ROWS * packed_half
        places = [(me, None)]
        for d in range(3):
            places += [(ups[d], has_up[d]), (downs[d], has_down[d])]
        for r, (place, there) in enumerate(places):
            row = row_of(owner_of(*place))
            if there is not None:
                row = jnp.where(there, row, -1)
            to_row = jnp.where(slots == r, row, to_row)
        row_choice[...] = to_row

    loads[5].wait()
    for side in range(2):
        x = (X - 1) * side
        for i, layer in enumerate((source[x], speed[0, x], pull[x], push[x], inverse[x])):
            layers[side, i] = layer

    for k in range(STAGES):
        for x in (0, X - 1):
            v = [fields[k, f, x] for f in range(F)]
            q = flux(v, joint_term(v, x), x, 0)
            for f in range(F):
                flux_x[k, x, f] = q[f]
        if k == 0:
            pl.semaphore_wait(barrier, expected)
        if k != 1:
            send_halo(k, 0)
        packs = [jnp.zeros((Y, Z), jnp.float32), jnp.zeros((Y, Z), jnp.float32)]
        for x in range(X):
            v = [fields[k, f, x] for f in range(F)]
            joint = joint_term(v, x)
            q = flux(v, joint, x, 2)
            columns = q + [source[x]] if k == 0 else q
            for f, column in enumerate(columns):
                here = lane == f * X + x
                packs[0] = jnp.where(here, jnp.broadcast_to(column[:, 0:1], (Y, Z)), packs[0])
                packs[1] = jnp.where(here, jnp.broadcast_to(column[:, Z - 1 : Z], (Y, Z)), packs[1])
            q = flux(v, joint, x, 1)
            for f in range(F):
                flux_y[k, f, pl.ds(x * Y, Y), :] = q[f]
            if k == 0:
                flux_y[k, F, pl.ds(x * Y, Y), :] = source[x]
        for side in range(2):
            send_z[k, side] = packs[side]
        send_halo(k, 2)
        for f in range(F + 1 if k == 0 else F):
            for side in range(2):
                send_y[k, side, f] = flux_y[k, f, pl.ds((Y - 1) * side, X, stride=Y), :]
        send_halo(k, 1)
        for x in range(X):
            v = [fields[k, f, x] for f in range(F)]
            joint = joint_term(v, x)
            if 0 < x < X - 1:
                q = flux(v, joint, x, 0)
                for f in range(F):
                    flux_x[k, x, f] = q[f]
            q = flux(v, joint, x, 2)
            for f in range(F):
                r = flux_y[k, f, pl.ds(x * Y, Y), :]
                fields[k + 1, f, x] = (
                    damp[x] * v[f]
                    + jnp.where(last_z, 0.0, pltpu.roll(q[f], Z - 1, 1))
                    - jnp.where(first_z, 0.0, pltpu.roll(q[f], 1, 1))
                ) + (
                    jnp.where(last_y, 0.0, pltpu.roll(r, Y - 1, 0))
                    - jnp.where(first_y, 0.0, pltpu.roll(r, 1, 0))
                )
        for x in range(X):
            for f in range(F):
                if x == 0:
                    fields[k + 1, f, x] += flux_x[k, x + 1, f]
                elif x == X - 1:
                    fields[k + 1, f, x] -= flux_x[k, x - 1, f]
                else:
                    fields[k + 1, f, x] += flux_x[k, x + 1, f] - flux_x[k, x - 1, f]
        if k == 0:
            each_side(lambda copy: copy.start(), True)
            send_tokens(1)
            loads[7].wait()
            loads[8].wait()
            route_tables()
            wait_tokens(1)
            send_tokens(2)
        if k < STAGES - 1:

            def add(f, x, delta):
                fields[k + 1, f, x] += delta

            def pass_line():
                wait_line(0)
                send_line(1)

            if k == 1:
                wait_tokens(2)
                send_line(0)
            finish_halo(k, add, pass_line if k == 1 else None)

    sixth = 0.5 * third
    tiles = []
    for f in range(F):
        total = jnp.zeros((Y, Z), jnp.float32)
        for x in range(X):
            value = third * fields[0, f, x] + 0.5 * fields[1, f, x] + sixth * fields[STAGES, f, x]
            result[f, x] = value
            total += value * source[x]
        weighted = [
            total,
            -sixth * flux_x[STAGES - 1, X - 1, f] * halo_layers[1, 0],
            sixth * flux_x[STAGES - 1, 0, f] * halo_layers[0, 0],
            -sixth * send_y[STAGES - 1, 1, f] * halo_y[0, 1, F],
            sixth * send_y[STAGES - 1, 0, f] * halo_y[0, 0, F],
        ]
        tile = jnp.zeros((TILE, Z), jnp.float32)
        for r, product in enumerate(weighted):
            line = jnp.sum(product, axis=0, keepdims=True)
            tile = jnp.where(row_index == r, jnp.broadcast_to(line, (TILE, Z)), tile)
        tiles.append(tile)

    block = jnp.zeros((TILE, Z), jnp.float32)
    for f in range(F):
        tile = tiles[f]
        for shift in (1, 2, 4, 8):
            tile = tile + pltpu.roll(tile, Z - shift, 1)
        if f:
            tile = pltpu.roll(tile, f, 1)
        block = jnp.where(lax.rem(lane, BZ) == f, tile, block)
    for side, row, sign in ((1, 5, -sixth), (0, 6, sixth)):
        shape = halo_z[0, side]
        shapes = jnp.zeros((Y, Z), jnp.float32)
        for f in range(F):
            moved = pltpu.roll(shape, Z - (F - f) * X, 1)
            shapes = jnp.where(lax.div(lane, X) == f, moved, shapes)
        line = jnp.broadcast_to(
            jnp.sum(sign * send_z[STAGES - 1, side] * shapes, axis=0, keepdims=True), (TILE, Z)
        )
        for shift in (1, 2, 4):
            line = line + pltpu.roll(line, Z - shift, 1)
        box = 0 if side else Z - BZ
        for f in range(F):
            moved = pltpu.roll(line, (box + f - f * X) % Z, 1)
            block = jnp.where(jnp.logical_and(row_index == row, lane == box + f), moved, block)
    block = step_length * block

    block = jnp.where(packed_half == 0, block[:ROWS], pltpu.roll(block, BZ // 2, 1)[ROWS:])
    to_row = row_choice[...]
    for t in range(n_row):
        row_send[t] = jnp.where(to_row == t, block, 0.0)

    def ring_copy(n, mine, device, src, dst, sems, r):
        t = lax.rem(mine + r, n)
        return pltpu.make_async_remote_copy(
            src_ref=src.at[t],
            dst_ref=dst.at[mine],
            send_sem=sems[0].at[r],
            recv_sem=sems[1].at[r],
            device_id=device(t),
            device_id_type=MESH,
        )

    row_copy = functools.partial(
        ring_copy, n_row, my_row, row_device, row_send, row_recv, (row_send_sem, row_recv_sem)
    )

    def cell_copy(dz, dy):
        return pltpu.make_async_remote_copy(
            src_ref=cell_send.at[cell_row(dz, dy)],
            dst_ref=cell_recv.at[my_cell],
            send_sem=cell_send_sem.at[dz * n_gz + dy],
            recv_sem=cell_recv_sem.at[dz * n_gz + dy],
            device_id=cell_device(dz, dy),
            device_id_type=MESH,
        )

    def far_first(n):
        return sorted(range(1, n), key=lambda r: -min(r, n - r))

    for r in far_first(n_row):
        row_copy(r).start()
    row_recv[my_row] = row_send[my_row]
    wait_line(1)
    send_line(2)
    for r in range(1, n_row):
        row_copy(r).wait_recv()
    rows = jnp.concatenate([row_recv[t] for t in range(n_row)], axis=0)
    parts = []
    for _ in range(PARTS):
        parts.append(rows.astype(jnp.bfloat16))
        rows = rows - parts[-1].astype(jnp.float32)
    cells = jnp.dot(
        choose[...], jnp.concatenate(parts, axis=0), preferred_element_type=jnp.float32
    )
    n_cell = n_gz * n_plane
    first_half = lax.rem(lax.broadcasted_iota(jnp.int32, (n_cell, Z), 1), BZ) < BZ // 2
    moved = jnp.where(first_half, 0.0, cells[n_cell:])
    cells = jnp.where(first_half, cells[:n_cell], 0.0) + pltpu.roll(moved, Z - BZ // 2, 1)
    for t in range(n_cell):
        cell_send[t] = cells[t : t + 1]
    wait_line(2)
    hops = [0] + far_first(n_gz)
    others = [(dz % n_plane, dy) for dz in range(1, n_plane + 1) for dy in hops]
    others.remove((0, 0))
    for dz, dy in others:
        cell_copy(dz, dy).start()
    cell_recv[my_cell] = cell_send[my_cell]

    def add_result(f, x, delta):
        result[f, x] += sixth * delta

    finish_halo(STAGES - 1, add_result)
    for k in range(STAGES):
        for d in range(3):
            for side, has in ((1, has_up[d]), (0, has_down[d])):

                @pl.when(has)
                def _(side=side, k=k, d=d):
                    halo_copy(k, d, side).wait_send()

    each_side(lambda copy: copy.wait_send(), True)

    for r in range(1, n_row):
        row_copy(r).wait_send()
    for dz, dy in others:
        cell_copy(dz, dy).wait_recv()
    own = jnp.sum(cell_recv[...].reshape(n_gz * n_plane, Z), axis=0, keepdims=True)
    grad_ref[...] = own
    for dz, dy in others:
        cell_copy(dz, dy).wait_send()


def write_out(fields, row, fields_out, gradient_out, gradient, sems):
    copy = pltpu.make_async_copy(fields, fields_out, sems.at[0])
    copy.start()
    to = lax.broadcasted_iota(jnp.int32, (TILE, Z), 1)
    place = BZ * lax.rem(to, BOXES) + lax.div(to, BOXES)
    wide = jnp.broadcast_to(row[...], (TILE, Z))
    gradient[...] = jnp.take_along_axis(wide, place, axis=1)[:1, : F * BOXES]
    small = pltpu.make_async_copy(gradient, gradient_out, sems.at[1])
    small.start()
    copy.wait()
    small.wait()


def solution(mesh):
    sizes = tuple(mesh.shape[axis] for axis in AXES)
    n_row = 2 * sizes[1]
    n_plane = sizes[0] // 2
    n_gz = sizes[2]

    def body(
        terminal_adjoint,
        density,
        velocity,
        stiffness,
        sponge,
        source_shape,
        brick_level,
        brick_patch,
        patch_owner,
    ):
        f32 = jnp.float32
        hbm = pl.BlockSpec(memory_space=pl.ANY)
        fields, gradient = pl.pallas_call(
            functools.partial(kernel, sizes),
            out_shape=(
                pltpu.VMEM((F, X, Y, Z), f32),
                pltpu.VMEM((1, Z), f32),
            ),
            in_specs=[hbm] * 9,
            out_specs=(pl.BlockSpec(memory_space=pltpu.VMEM),) * 2,
            scratch_shapes=[
                pltpu.SMEM((sizes[1], sizes[2], sizes[0]), jnp.int32),
                pltpu.SMEM((sizes[1], sizes[2], sizes[0]), jnp.int32),
                pltpu.SMEM((sizes[0] * sizes[1] * sizes[2],), jnp.int32),
                pltpu.VMEM((STAGES + 1, F, X, Y, Z), f32),
                pltpu.VMEM((X, Y, Z), f32),
                pltpu.VMEM((3, X, Y, Z), f32),
                pltpu.VMEM((X, Y, Z), f32),
                pltpu.VMEM((X, Y, Z), f32),
                pltpu.VMEM((X, Y, Z), f32),
                pltpu.VMEM((3, X, Y, Z), f32),
                pltpu.VMEM((X, Y, Z), f32),
                pltpu.VMEM((X, Y, Z), f32),
                pltpu.VMEM((X, Y, Z), f32),
                pltpu.VMEM((X, Y, Z), f32),
                pltpu.VMEM((STAGES, X, F, Y, Z), f32),
                pltpu.VMEM((STAGES, F + 1, X * Y, Z), f32),
                pltpu.VMEM((STAGES, 2, F + 1, X, Z), f32),
                pltpu.VMEM((STAGES, 2, Y, Z), f32),
                pltpu.VMEM((STAGES, 2, F, Y, Z), f32),
                pltpu.VMEM((STAGES, 2, F + 1, X, Z), f32),
                pltpu.VMEM((STAGES, 2, Y, Z), f32),
                pltpu.VMEM((2, F, Y, Z), f32),
                pltpu.VMEM((2, LAYERS, Y, Z), f32),
                pltpu.VMEM((2, LAYERS, Y, Z), f32),
                pltpu.VMEM((2 * n_plane * n_gz, PARTS * n_row * ROWS), jnp.bfloat16),
                pltpu.VMEM((ROWS, Z), jnp.int32),
                pltpu.VMEM((n_row, ROWS, Z), f32),
                pltpu.VMEM((n_row, ROWS, Z), f32),
                pltpu.VMEM((n_plane * n_gz, 1, Z), f32),
                pltpu.VMEM((n_plane * n_gz, 1, Z), f32),
                pltpu.SemaphoreType.DMA((9,)),
                pltpu.SemaphoreType.DMA((STAGES, 3, 2)),
                pltpu.SemaphoreType.DMA((STAGES, 3, 2)),
                pltpu.SemaphoreType.DMA((2,)),
                pltpu.SemaphoreType.DMA((2,)),
                pltpu.SemaphoreType.DMA((n_row,)),
                pltpu.SemaphoreType.DMA((n_row,)),
                pltpu.SemaphoreType.DMA((n_plane * n_gz,)),
                pltpu.SemaphoreType.DMA((n_plane * n_gz,)),
                pltpu.SemaphoreType.REGULAR((2, 2)),
                pltpu.SemaphoreType.REGULAR((3,)),
            ],
            compiler_params=pltpu.CompilerParams(collective_id=0, has_side_effects=True),
        )(
            jnp.transpose(brick_level, (1, 2, 0)),
            jnp.transpose(brick_patch, (1, 2, 0)),
            patch_owner,
            terminal_adjoint,
            density,
            velocity,
            stiffness,
            sponge,
            source_shape,
        )
        return pl.pallas_call(
            write_out,
            out_shape=(
                jax.ShapeDtypeStruct((F, X, Y, Z), f32),
                jax.ShapeDtypeStruct((1, F * BOXES), f32),
            ),
            in_specs=[pl.BlockSpec(memory_space=pltpu.VMEM)] * 2,
            out_specs=(hbm, hbm),
            scratch_shapes=[pltpu.VMEM((1, F * BOXES), f32), pltpu.SemaphoreType.DMA((2,))],
        )(
            pltpu.with_memory_space_constraint(fields, pltpu.VMEM),
            pltpu.with_memory_space_constraint(gradient, pltpu.VMEM),
        )

    in_specs = (
        P(None, "gx", "gy", "gz"),
        P("gx", "gy", "gz"),
        P(None, "gx", "gy", "gz"),
        P("gx", "gy", "gz"),
        P("gx", "gy", "gz"),
        P("gx", "gy", "gz"),
        P(),
        P(),
        P(),
    )
    out_specs = (P(None, "gx", "gy", "gz"), P(AXES, None))
    return jax.shard_map(body, mesh=mesh, in_specs=in_specs, out_specs=out_specs, check_vma=False)
```
